256 devices in a mesh: layer: 8 (over y_lo, x), prow: 4 (over y_hi, core), pcol: 8 (over z).
Axes of the slice: x: 4, y: 4 (y_hi: 2, y_lo: 2; y = y_hi * 2 + y_lo), z: 8, core: 2. Of those that a mesh axis runs over, the one named last changes fastest.
Arguments:
- front_blocks: float32 [8, 4, 1024, 4, 1024], P('layer', None, 'prow', None, 'pcol'), may hold values from -6 to 6, as said below
- fill_mask: int32 [32, 32], replicated, may hold values from 0 to 1, as said below
Outputs:
- factored: float32 [8, 4, 1024, 4, 1024], P('layer', None, 'prow', None, 'pcol')
- ancestor: float32 [3, 4, 8, 32, 3, 1024], P(None, 'prow', 'layer', None, None, 'pcol')
The draws below stay inside these ranges and needn't reach their ends.
Inputs may be any that keep to these rules, and one draw needn't show every extreme that they name: `front_blocks`: with the fill pattern applied, every pivot block that the elimination meets is invertible and well conditioned. `fill_mask`: block row i is filled exactly from some block column at most i // 2 through the diagonal block, and block column j exactly from some block row at most j // 2 through the diagonal block; all other block pairs are empty.
All inputs are finite; a program needn't handle non-finite values.
Results may differ from the reference program's by a relative error of at most 0.0001.
Values sent between devices are 32-bit elements; how exact they have to be, the bound alone decides.
A program may use at most 128 MiB of HBM per device.

```python
import jax
import jax.numpy as jnp
from jax import lax

F = 4096
P_SIZE = 1024
BS = 128
PANELS = 1
LAYERS = 8
GRID_ROWS = 4
NS = 4
NA = 3
RL = 32


def fill_parts(key):
    blocks_count = F // BS
    index_row = jnp.arange(blocks_count, dtype=jnp.int32)
    row_first = jax.random.randint(jax.random.fold_in(key, 21), (blocks_count,), 0, index_row // 2 + 1)
    column_first = jax.random.randint(jax.random.fold_in(key, 22), (blocks_count,), 0, index_row // 2 + 1)
    below_part = (index_row[None, :] >= row_first[:, None]) & (index_row[None, :] <= index_row[:, None])
    above_part = (index_row[:, None] >= column_first[None, :]) & (index_row[:, None] < index_row[None, :])
    return (below_part, above_part)


def expand_blocks(block_table):
    return jnp.repeat(jnp.repeat(block_table.astype(jnp.float32), BS, axis=0), BS, axis=1)


def draw_front_blocks(key, part):
    below_part, above_part = fill_parts(key)
    order_full = NS * P_SIZE
    blocks_count = F // BS
    diagonal_blocks = jnp.eye(blocks_count, dtype=jnp.bool_)
    lower_allowed = expand_blocks(below_part)
    upper_allowed = expand_blocks(above_part | diagonal_blocks)
    outside = 1.0 - expand_blocks(below_part | above_part)
    position = jnp.arange(order_full, dtype=jnp.int32)
    strict_lower = (position[:, None] > position[None, :]).astype(jnp.float32)
    strict_upper = (position[:, None] < position[None, :]).astype(jnp.float32)
    same_block = position[:, None] // BS == position[None, :] // BS
    spread = jnp.where(same_block, 0.6 / jnp.sqrt(jnp.float32(BS)), 1.5 / jnp.sqrt(jnp.float32(order_full)))
    outer_scale = 1.5 / jnp.sqrt(jnp.float32(order_full))
    lower_shape = spread * lower_allowed * strict_lower
    upper_shape = spread * upper_allowed * strict_upper
    layer_keys = jax.random.split(jax.random.fold_in(key, 11), LAYERS)

    def one_layer(layer_key):
        key_lower = jax.random.fold_in(layer_key, 1)
        key_upper = jax.random.fold_in(layer_key, 2)
        key_gain = jax.random.fold_in(layer_key, 3)
        key_outer = jax.random.fold_in(layer_key, 4)
        shape_full = (order_full, order_full)
        noise_lower = jax.random.truncated_normal(key_lower, -4.0, 4.0, shape_full, jnp.float32)
        noise_upper = jax.random.truncated_normal(key_upper, -4.0, 4.0, shape_full, jnp.float32)
        noise_outer = jax.random.truncated_normal(key_outer, -4.0, 4.0, shape_full, jnp.float32)
        gains = jax.random.uniform(key_gain, (order_full,), jnp.float32, 1.2, 2.0)
        lower_factor = jnp.eye(order_full, dtype=jnp.float32) + noise_lower * lower_shape
        upper_factor = jnp.diag(gains) + noise_upper * upper_shape
        product = jnp.dot(lower_factor, upper_factor, precision=lax.Precision.HIGHEST, preferred_element_type=jnp.float32)
        return product + noise_outer * outer_scale * outside
    matrices = lax.map(one_layer, layer_keys)
    return matrices.reshape(LAYERS, NS, P_SIZE, NS, P_SIZE)


def draw_fill_mask(key, part):
    below_part, above_part = fill_parts(key)
    return (below_part | above_part).astype(jnp.int32)


def setup_inputs(seed: int = 0) -> dict:
    arg_keys = jax.random.split(jax.random.key(seed), 3)
    front_blocks = draw_front_blocks(jax.random.fold_in(arg_keys[2], 71), 0)
    fill_mask = draw_fill_mask(jax.random.fold_in(arg_keys[2], 71), 0)
    return dict(front_blocks=front_blocks, fill_mask=fill_mask)


def full_dot(left, right):
    return jnp.dot(left.astype(jnp.float32), right.astype(jnp.float32), precision=lax.Precision.HIGHEST, preferred_element_type=jnp.float32)

def reference(front_blocks, fill_mask):
    fill_full = jnp.repeat(jnp.repeat(fill_mask.astype(jnp.float32), BS, axis=0), BS, axis=1)

    def eliminate(layer_front):
        matrix = layer_front.reshape(F, F) * fill_full
        for column in range(PANELS * P_SIZE // BS):
            begin_at = column * BS
            end_at = begin_at + BS
            inverse = jnp.linalg.inv(matrix[begin_at:end_at, begin_at:end_at])
            lower_part = full_dot(matrix[end_at:, begin_at:end_at], inverse)
            matrix = matrix.at[end_at:, begin_at:end_at].set(lower_part)
            matrix = matrix.at[end_at:, end_at:].add(-full_dot(lower_part, matrix[begin_at:end_at, end_at:]))
        return matrix
    factored = lax.map(eliminate, front_blocks)
    edge_index = PANELS * P_SIZE
    summed = jnp.sum(factored[:, edge_index:, edge_index:], axis=0)
    return (factored.reshape(LAYERS, NS, P_SIZE, NS, P_SIZE), summed.reshape(NA, GRID_ROWS, LAYERS, RL, NA, P_SIZE))
```

```python
import jax
import jax.numpy as jnp
from jax import lax
from jax.experimental import pallas as pl
from jax.experimental.pallas import tpu as pltpu
from jax.sharding import PartitionSpec as P

BS = 128
MESH = pl.DeviceIdType.MESH


def dot(left, right, dims=((1,), (0,)), precision=lax.Precision.HIGHEST):
    return lax.dot_general(
        left, right, (dims, ((), ())), precision=precision, preferred_element_type=jnp.float32
    )


def bulk(left, right):
    return dot(left, right, precision=lax.Precision.HIGH)


def lanes_of(block, column):
    return jnp.broadcast_to(block[:, column : column + 1], (8, BS))


def row_of(block, row):
    return jnp.broadcast_to(block[row : row + 1, :], (8, BS))


def invert(pivot, unit_ref, scaled_ref):
    gram = dot(pivot, pivot, ((1,), (1,)))
    groups = [gram[8 * p : 8 * p + 8, :] for p in range(BS // 8)]
    lane = lax.broadcasted_iota(jnp.int32, (8, BS), 1)
    sub = lax.broadcasted_iota(jnp.int32, (8, BS), 0)
    for p in range(BS // 8):
        rows = groups[p]
        own = (lane >= 8 * p) & (lane < 8 * p + 8)
        eye = jnp.where(lane - 8 * p == sub, 1.0, 0.0)
        columns = [lanes_of(rows, 8 * p + j) for j in range(8)]
        unit_ref[8 * p : 8 * p + 8, :] = jnp.where(lane < 8 * p, rows, eye)
        rows = jnp.where(own, eye, rows)
        for k in range(8):
            at = sub == k
            factor = columns[k]
            scale = 1.0 / row_of(factor, k)
            top = row_of(rows, k)
            rows = jnp.where(at, top * scale, rows - (factor * top) * scale)
            for j in range(k + 1, 8):
                top = row_of(columns[j], k)
                columns[j] = jnp.where(at, top * scale, columns[j] - (factor * top) * scale)
        scaled_ref[8 * p : 8 * p + 8, :] = jnp.where(lane < 8 * p + 8, rows, 0.0)
        tops = [row_of(rows, k) for k in range(8)]
        for q in range(p + 1, BS // 8):
            term = [lanes_of(groups[q], 8 * p + k) * tops[k] for k in range(8)]
            total = ((term[0] + term[1]) + (term[2] + term[3])) + ((term[4] + term[5]) + (term[6] + term[7]))
            groups[q] = jnp.where(own, 0.0, groups[q]) - total
    right = dot(unit_ref[...], pivot)
    return dot(right, scaled_ref[...], ((0,), (0,)))


def kernel(
    x_ref, mask_ref, out_ref, anc_ref,
    praw, uraw, lraw, work, low, tail, got, inv, unit, scaled,
    send, recv, near, far, up_send, up_recv, lo_send, lo_recv, sum_send, sum_recv, local,
):
    layer, row, col = lax.axis_index("layer"), lax.axis_index("prow"), lax.axis_index("pcol")
    cols, rows_n, layers = 8, 4, 8
    mate = row + 1 - 2 * lax.rem(row, 2)
    over = lax.rem(row + 2, rows_n)
    right, left = lax.rem(col + 1, cols), lax.rem(col + cols - 1, cols)

    own = [
        pltpu.make_async_copy(x_ref.at[0, pl.ds(0, 256), :], praw.at[row, col], local.at[0]),
        pltpu.make_async_copy(x_ref.at[0, pl.ds(256, 768), :], lraw.at[col], local.at[1]),
        pltpu.make_async_copy(x_ref.at[pl.ds(1, 3), pl.ds(0, 256), :], uraw.at[row], local.at[2]),
    ]
    for copy in own:
        copy.start()

    barrier = pltpu.get_barrier_semaphore()

    def greet(*device):
        pl.semaphore_signal(barrier, inc=1, device_id=device, device_id_type=MESH)

    greet(layer, mate, col)
    greet(layer, over, col)
    greet(layer, row, right)
    greet(layer, row, left)
    for d in range(1, layers):
        greet(lax.rem(layer + d, layers), row, col)
    pl.semaphore_wait(barrier, 4 + layers - 1)

    def remote(src, dst, send_sem, recv_sem, *device):
        return pltpu.make_async_remote_copy(
            src_ref=src, dst_ref=dst, send_sem=send_sem, recv_sem=recv_sem,
            device_id=device, device_id_type=MESH,
        )

    sent = []

    def go(copy):
        copy.start()
        sent.append(copy)

    groups = (row, over)
    limit = ((4, 3), (3, 4))
    tile = x_ref.at[0, pl.ds(0, 256), :]
    step_to = (right, left)

    def origin(way, hop):
        return lax.rem(col + (cols - hop if way == 0 else hop), cols)

    go(remote(tile, praw.at[row, col], near.at[0], near.at[1], layer, over, col))
    for way in range(2):
        go(remote(tile, praw.at[row, col], send.at[0, way, 0], recv.at[0, way, 0], layer, row, step_to[way]))
    go(remote(tile, praw.at[row, col], near.at[2], near.at[3], layer, mate, col))
    blocks = x_ref.at[pl.ds(1, 3), pl.ds(0, 256), :]
    go(remote(blocks, uraw.at[row], up_send.at[0], up_recv.at[0], layer, over, col))
    go(remote(blocks, uraw.at[row], up_send.at[1], up_recv.at[1], layer, mate, col))
    for copy in own:
        copy.wait()

    place = praw.at[over, col]
    remote(place, place, near.at[0], near.at[1], layer, over, col).wait_recv()
    for way in range(2):
        go(remote(place, place, send.at[1, way, 0], recv.at[1, way, 0], layer, row, step_to[way]))
    go(remote(place, place, near.at[4], near.at[5], layer, mate, col))

    for hop in range(1, 5):
        for kind in range(2):
            for way in range(2):
                if hop > limit[kind][way]:
                    continue
                place = praw.at[groups[kind], origin(way, hop)]
                remote(
                    place, place, send.at[kind, way, hop - 1], recv.at[kind, way, hop - 1],
                    layer, row, step_to[way],
                ).wait_recv()
                if hop < limit[kind][way]:
                    go(remote(
                        place, place, send.at[kind, way, hop], recv.at[kind, way, hop],
                        layer, row, step_to[way],
                    ))
                go(remote(
                    place, place, far.at[0, kind, way, hop - 1], far.at[1, kind, way, hop - 1],
                    layer, mate, col,
                ))

    def low_part(kind, source):
        return lraw.at[source, pl.ds(384 * kind, 384), :]

    for kind in range(2):
        for way in range(2):
            half = x_ref.at[0, pl.ds(256 + 384 * kind, 384), :]
            go(remote(
                half, low_part(kind, col), lo_send.at[kind, way, 0], lo_recv.at[kind, way, 0],
                layer, row, step_to[way],
            ))

    def low_hop(hop):
        for kind in range(2):
            for way in range(2):
                if hop > limit[kind][way]:
                    continue
                place = low_part(kind, origin(way, hop))
                remote(
                    place, place, lo_send.at[kind, way, hop - 1], lo_recv.at[kind, way, hop - 1],
                    layer, row, step_to[way],
                ).wait_recv()
                if hop < limit[kind][way]:
                    remote(
                        place, place, lo_send.at[kind, way, hop], lo_recv.at[kind, way, hop],
                        layer, row, step_to[way],
                    ).start()

    mates = (mate, rows_n - 1 - row)
    place = praw.at[mates[0], col]
    remote(place, place, near.at[2], near.at[3], layer, mate, col).wait_recv()
    place = praw.at[mates[1], col]
    remote(place, place, near.at[4], near.at[5], layer, mate, col).wait_recv()
    place = uraw.at[over]
    remote(place, place, up_send.at[0], up_recv.at[0], layer, over, col).wait_recv()
    go(remote(place, place, up_send.at[2], up_recv.at[2], layer, mate, col))
    for hop in range(1, 5):
        for kind in range(2):
            for way in range(2):
                if hop > limit[kind][way]:
                    continue
                place = praw.at[mates[kind], origin(way, hop)]
                remote(
                    place, place, far.at[0, kind, way, hop - 1], far.at[1, kind, way, hop - 1],
                    layer, mate, col,
                ).wait_recv()
    place = uraw.at[mates[0]]
    remote(place, place, up_send.at[1], up_recv.at[1], layer, mate, col).wait_recv()
    place = uraw.at[mates[1]]
    remote(place, place, up_send.at[2], up_recv.at[2], layer, mate, col).wait_recv()

    def filled(i, j):
        return mask_ref[i, j].astype(jnp.float32)

    @pl.loop(0, 8)
    def _(i):
        group, part = i // 2, pl.multiple_of(lax.rem(i, 2) * BS, BS)
        here = pl.ds(pl.multiple_of(i * BS, BS), BS)
        for j in range(8):
            work[here, j * BS : (j + 1) * BS] = praw[group, j, pl.ds(part, BS), :] * filled(i, j)
        for b in range(3):
            work[here, 1024 + b * BS : 1024 + (b + 1) * BS] = (
                uraw[group, b, pl.ds(part, BS), :] * filled(i, 8 * (b + 1) + col)
            )

    @pl.loop(0, 8)
    def _(j):
        here = pl.ds(pl.multiple_of(j * BS, BS), BS)
        inv[j] = invert(work[here, here], unit, scaled)
        for k in range(7):

            @pl.when(j == k)
            def _(k=k):
                begin, end = k * BS, (k + 1) * BS
                factors = bulk(work[end:1024, begin:end], inv[k])
                work[end:1024, begin:end] = factors
                for start in range(end, 1408, 256):
                    stop = min(start + 256, 1408)
                    work[end:1024, start:stop] -= bulk(factors, work[begin:end, start:stop])

        for hop in range(1, 5):

            @pl.when(j == 2 * hop - 1)
            def _(hop=hop):
                low_hop(hop)

    @pl.loop(0, 6)
    def _(i):
        here = pl.ds(pl.multiple_of(i * BS, BS), BS)
        block_row = 8 * (i // 2 + 1) + 2 * row + lax.rem(i, 2)
        for j in range(8):
            low[here, j * BS : (j + 1) * BS] = lraw[j, here, :] * filled(block_row, j)

    for k in range(8):
        begin, end = k * BS, (k + 1) * BS
        rest = low[:, begin:end]
        if k:
            rest = rest - bulk(low[:, :begin], work[:begin, begin:end])
        low[:, begin:end] = bulk(rest, inv[k])

    for a in range(3):
        here = slice(256 * a, 256 * a + 256)
        term = bulk(low[here, :], work[:, 1024:1408])
        for h in range(2):
            for b in range(3):
                block = x_ref[b + 1, 256 * (a + 1) + BS * h : 256 * (a + 1) + BS * (h + 1), :]
                block = block * filled(8 * (a + 1) + 2 * row + h, 8 * (b + 1) + col)
                block = block - term[BS * h : BS * (h + 1), BS * b : BS * (b + 1)]
                tail[a, BS * h : BS * (h + 1), BS * b : BS * (b + 1)] = block
        for d in range(1, layers):
            other = lax.rem(layer + d, layers)
            go(remote(
                tail.at[a, pl.ds(pl.multiple_of(other * 32, 32), 32), :], got.at[d, a],
                sum_send.at[d, a], sum_recv.at[d, a], other, row, col,
            ))

    mine, there = pl.ds(pl.multiple_of(row * 256, 256), 256), pl.ds(pl.multiple_of(col * BS, BS), BS)
    out_ref[pl.ds(0, 256, stride=4), :] = work[mine, there]
    for b in range(3):
        out_ref[pl.ds(b + 1, 256, stride=4), :] = work[mine, 1024 + BS * b : 1024 + BS * (b + 1)]
    for a in range(3):
        base = 1024 * (a + 1)
        out_ref[pl.ds(base, 256, stride=4), :] = low[256 * a : 256 * (a + 1), there]
        for b in range(3):
            out_ref[pl.ds(base + b + 1, 256, stride=4), :] = tail[a, :, BS * b : BS * (b + 1)]

    ours = pl.ds(pl.multiple_of(layer * 32, 32), 32)
    for a in range(3):
        for d in range(1, layers):
            place = got.at[d, a]
            remote(place, place, sum_send.at[d, a], sum_recv.at[d, a], layer, row, col).wait_recv()
        total = tail[a, ours, :]
        for d in range(1, layers):
            total = total + got[d, a]
        for b in range(3):
            anc_ref[pl.ds(96 * a + b, 32, stride=3), :] = total[:, BS * b : BS * (b + 1)]

    for copy in sent:
        copy.wait_send()
    for kind in range(2):
        for way in range(2):
            for hop in range(1, limit[kind][way]):
                place = low_part(kind, col)
                remote(
                    place, place, lo_send.at[kind, way, hop], lo_recv.at[kind, way, hop],
                    layer, row, step_to[way],
                ).wait_send()


def on_device(front_blocks, fill_mask):
    tiles = front_blocks[0].transpose(2, 0, 1, 3).reshape(4, 1024, 128)
    dma = pltpu.SemaphoreType.DMA
    vmem = lambda *shape: pltpu.VMEM(shape, jnp.float32)
    factored, ancestor = pl.pallas_call(
        kernel,
        out_shape=(
            jax.ShapeDtypeStruct((4096, 128), jnp.float32),
            jax.ShapeDtypeStruct((288, 128), jnp.float32),
        ),
        in_specs=[pl.BlockSpec(memory_space=pltpu.VMEM), pl.BlockSpec(memory_space=pltpu.SMEM)],
        out_specs=(pl.BlockSpec(memory_space=pltpu.VMEM), pl.BlockSpec(memory_space=pltpu.VMEM)),
        scratch_shapes=[
            vmem(4, 8, 256, 128), vmem(4, 3, 256, 128), vmem(8, 768, 128),
            vmem(1024, 1408), vmem(768, 1024), vmem(3, 256, 384), vmem(8, 3, 32, 384),
            vmem(8, 128, 128), vmem(128, 128), vmem(128, 128),
            dma((2, 2, 4)), dma((2, 2, 4)), dma((6,)), dma((2, 2, 2, 4)),
            dma((3,)), dma((3,)), dma((2, 2, 4)), dma((2, 2, 4)), dma((8, 3)), dma((8, 3)), dma((3,)),
        ],
        compiler_params=pltpu.CompilerParams(
            collective_id=0, has_side_effects=True, vmem_limit_bytes=60 * 1024 * 1024
        ),
        name="eliminate",
    )(tiles, fill_mask)
    return factored.reshape(1, 4, 256, 4, 128), ancestor.reshape(3, 1, 1, 32, 3, 128)


def solution(mesh):
    split = P("layer", None, "prow", None, "pcol")
    return jax.shard_map(
        on_device,
        mesh=mesh,
        in_specs=(split, P()),
        out_specs=(split, P(None, "prow", "layer", None, None, "pcol")),
        check_vma=False,
    )
```

```python
import jax
import jax.numpy as jnp
from jax import lax
from jax.experimental import pallas as pl
from jax.experimental.pallas import tpu as pltpu
from jax.sharding import PartitionSpec as P

BS = 128
LATE = 3
MESH = pl.DeviceIdType.MESH


def dot(left, right, dims=((1,), (0,)), precision=lax.Precision.HIGHEST):
    return lax.dot_general(
        left, right, (dims, ((), ())), precision=precision, preferred_element_type=jnp.float32
    )


def bulk(left, right):
    return dot(left, right, precision=lax.Precision.HIGH)


def lanes_of(block, column):
    return jnp.broadcast_to(block[:, column : column + 1], (8, BS))


def row_of(block, row):
    return jnp.broadcast_to(block[row : row + 1, :], (8, BS))


def invert(pivot, unit_ref, scaled_ref):
    gram = dot(pivot, pivot, ((1,), (1,)))
    count = BS // 8
    half = count // 2
    groups = [gram[8 * p : 8 * p + 8, :] for p in range(count)]
    lane = lax.broadcasted_iota(jnp.int32, (8, BS), 1)
    sub = lax.broadcasted_iota(jnp.int32, (8, BS), 0)
    raw, done = [], []
    for p in range(count):
        if p == half:
            term = dot(jnp.concatenate(raw, 0), jnp.concatenate(done, 0), ((0,), (0,)))
            for q in range(half, count):
                groups[q] = jnp.where(lane < 8 * half, 0.0, groups[q]) - term[8 * q : 8 * q + 8, :]
        rows = groups[p]
        raw.append(rows)
        own = (lane >= 8 * p) & (lane < 8 * p + 8)
        eye = jnp.where(lane - 8 * p == sub, 1.0, 0.0)
        columns = [lanes_of(rows, 8 * p + j) for j in range(8)]
        unit_ref[8 * p : 8 * p + 8, :] = jnp.where(lane < 8 * p, rows, eye)
        rows = jnp.where(own, eye, rows)
        for k in range(0, 8, 2):
            first, second = columns[k], columns[k + 1]
            a, b = row_of(first, k), row_of(second, k)
            c, d = row_of(first, k + 1), row_of(second, k + 1)
            scale = 1.0 / (a * d - b * c)
            at, after = sub == k, sub == k + 1
            left = jnp.where(at, -d, jnp.where(after, c, first * d - second * c))
            right = jnp.where(at, b, jnp.where(after, -a, second * a - first * b))

            def cleared(block, k=k, pair=at | after, left=left, right=right, scale=scale):
                term = left * row_of(block, k) + right * row_of(block, k + 1)
                return jnp.where(pair, 0.0, block) - term * scale

            rows = cleared(rows)
            for j in range(k + 2, 8):
                columns[j] = cleared(columns[j])
        end = 8 * half if p < half else BS
        done.append(jnp.where((lane < 8 * p + 8) | (lane >= end), rows, 0.0))
        scaled_ref[8 * p : 8 * p + 8, :] = jnp.where(lane < 8 * p + 8, rows, 0.0)
        tops = [row_of(rows, k) for k in range(8)]
        for q in range(p + 1, half if p < half else count):
            term = [lanes_of(groups[q], 8 * p + k) * tops[k] for k in range(8)]
            total = ((term[0] + term[1]) + (term[2] + term[3])) + ((term[4] + term[5]) + (term[6] + term[7]))
            groups[q] = jnp.where(own, 0.0, groups[q]) - total
    right = dot(unit_ref[...], pivot)
    return dot(right, scaled_ref[...], ((0,), (0,)))


def halves(value):
    high = value.astype(jnp.bfloat16)
    return high, (value - high.astype(jnp.float32)).astype(jnp.bfloat16)


def passes(left, right):
    def one(a, b):
        return jnp.dot(a, b, preferred_element_type=jnp.float32)

    return one(left[0], right[0]) + (one(left[0], right[1]) + one(left[1], right[0]))


def kernel(
    x_ref, mask_ref, out_ref, anc_ref,
    praw, uraw, lraw, rest, work, low, low_high, low_low, up_high, up_low, pairs, tail, got, inv, unit, scaled,
    send, recv, near, far, up_send, up_recv, lo_send, lo_recv, sum_send, sum_recv, local,
):
    layer, row, col = lax.axis_index("layer"), lax.axis_index("prow"), lax.axis_index("pcol")
    cols, rows_n, layers = 8, 4, 8
    mate = row + 1 - 2 * lax.rem(row, 2)
    over = lax.rem(row + 2, rows_n)
    right, left = lax.rem(col + 1, cols), lax.rem(col + cols - 1, cols)

    own = [pltpu.make_async_copy(x_ref.at[0, :, 0, :], praw.at[row, col], local.at[0])]
    for a in range(3):
        own.append(pltpu.make_async_copy(x_ref.at[a + 1, :, 0, :], lraw.at[col, pl.ds(256 * a, 256), :], local.at[1 + a]))
        own.append(pltpu.make_async_copy(x_ref.at[0, :, a + 1, :], uraw.at[row, a], local.at[4 + a]))
    trailing = [
        pltpu.make_async_copy(x_ref.at[a + 1, :, b + 1, :], rest.at[a, b], local.at[7 + 3 * a + b])
        for a in range(3)
        for b in range(3)
    ]
    for copy in own + trailing:
        copy.start()

    barrier = pltpu.get_barrier_semaphore()

    def greet(*device):
        pl.semaphore_signal(barrier, inc=1, device_id=device, device_id_type=MESH)

    greet(layer, mate, col)
    greet(layer, over, col)
    greet(layer, row, right)
    greet(layer, row, left)
    for d in range(1, layers):
        greet(lax.rem(layer + d, layers), row, col)
    pl.semaphore_wait(barrier, 4 + layers - 1)

    for copy in own:
        copy.wait()

    def remote(src, dst, send_sem, recv_sem, *device):
        return pltpu.make_async_remote_copy(
            src_ref=src, dst_ref=dst, send_sem=send_sem, recv_sem=recv_sem,
            device_id=device, device_id_type=MESH,
        )

    sent = []

    def go(copy):
        copy.start()
        sent.append(copy)

    groups = (row, over)
    limit = ((4, 3), (3, 4))
    tile = praw.at[row, col]
    step_to = (right, left)

    def origin(way, hop):
        return lax.rem(col + (cols - hop if way == 0 else hop), cols)

    go(remote(tile, tile, near.at[0], near.at[1], layer, over, col))
    for way in range(2):
        go(remote(tile, tile, send.at[0, way, 0], recv.at[0, way, 0], layer, row, step_to[way]))
    go(remote(tile, tile, near.at[2], near.at[3], layer, mate, col))
    blocks = uraw.at[row]
    go(remote(blocks, blocks, up_send.at[0], up_recv.at[0], layer, over, col))
    place = praw.at[over, col]
    remote(place, place, near.at[0], near.at[1], layer, over, col).wait_recv()
    for way in range(2):
        go(remote(place, place, send.at[1, way, 0], recv.at[1, way, 0], layer, row, step_to[way]))
    go(remote(place, place, near.at[4], near.at[5], layer, mate, col))

    for hop in range(1, 5):
        for kind in range(2):
            for way in range(2):
                if hop > limit[kind][way]:
                    continue
                place = praw.at[groups[kind], origin(way, hop)]
                remote(
                    place, place, send.at[kind, way, hop - 1], recv.at[kind, way, hop - 1],
                    layer, row, step_to[way],
                ).wait_recv()
                if hop < limit[kind][way]:
                    go(remote(
                        place, place, send.at[kind, way, hop], recv.at[kind, way, hop],
                        layer, row, step_to[way],
                    ))
                go(remote(
                    place, place, far.at[0, kind, way, hop - 1], far.at[1, kind, way, hop - 1],
                    layer, mate, col,
                ))

    def low_part(kind, source):
        return lraw.at[source, pl.ds(384 * kind, 384), :]

    for kind in range(2):
        for way in range(2):
            half = low_part(kind, col)
            go(remote(
                half, half, lo_send.at[kind, way, 0], lo_recv.at[kind, way, 0],
                layer, row, step_to[way],
            ))

    def low_hop(hop):
        for kind in range(2):
            for way in range(2):
                if hop > limit[kind][way]:
                    continue
                place = low_part(kind, origin(way, hop))
                remote(
                    place, place, lo_send.at[kind, way, hop - 1], lo_recv.at[kind, way, hop - 1],
                    layer, row, step_to[way],
                ).wait_recv()
                if hop < limit[kind][way]:
                    remote(
                        place, place, lo_send.at[kind, way, hop], lo_recv.at[kind, way, hop],
                        layer, row, step_to[way],
                    ).start()

    mates = (mate, rows_n - 1 - row)
    place = praw.at[mates[0], col]
    remote(place, place, near.at[2], near.at[3], layer, mate, col).wait_recv()
    place = praw.at[mates[1], col]
    remote(place, place, near.at[4], near.at[5], layer, mate, col).wait_recv()
    go(remote(blocks, blocks, up_send.at[1], up_recv.at[1], layer, mate, col))
    for hop in range(1, 5):
        for kind in range(2):
            for way in range(2):
                if hop > limit[kind][way]:
                    continue
                place = praw.at[mates[kind], origin(way, hop)]
                remote(
                    place, place, far.at[0, kind, way, hop - 1], far.at[1, kind, way, hop - 1],
                    layer, mate, col,
                ).wait_recv()
    def up_over():
        place = uraw.at[over]
        remote(place, place, up_send.at[0], up_recv.at[0], layer, over, col).wait_recv()
        remote(place, place, up_send.at[2], up_recv.at[2], layer, mate, col).start()

    def up_here():
        for k in range(2):
            place = uraw.at[mates[k]]
            remote(place, place, up_send.at[1 + k], up_recv.at[1 + k], layer, mate, col).wait_recv()
        for i in range(8):
            for b in range(3):
                work[i * BS : (i + 1) * BS, 1024 + b * BS : 1024 + (b + 1) * BS] = (
                    uraw[i // 2, b, (i % 2) * BS : (i % 2 + 1) * BS, :] * filled(i, 8 * (b + 1) + col)
                )
        for k in range(LATE):
            begin, end = k * BS, (k + 1) * BS
            work[end:1024, 1024:1408] -= bulk(work[end:1024, begin:end], work[begin:end, 1024:1408])

    def filled(i, j):
        return mask_ref[i, j].astype(jnp.float32)

    @pl.loop(0, 8)
    def _(i):
        group, part = i // 2, pl.multiple_of(lax.rem(i, 2) * BS, BS)
        here = pl.ds(pl.multiple_of(i * BS, BS), BS)
        for j in range(8):
            work[here, j * BS : (j + 1) * BS] = praw[group, j, pl.ds(part, BS), :] * filled(i, j)

    @pl.loop(0, 8)
    def _(j):
        here = pl.ds(pl.multiple_of(j * BS, BS), BS)
        inv[j] = invert(work[here, here], unit, scaled)
        pl.when(j == 1)(up_over)
        pl.when(j == LATE)(up_here)
        for k in range(7):

            @pl.when(j == k)
            def _(k=k):
                begin, end = k * BS, (k + 1) * BS
                factors = bulk(work[end:1024, begin:end], inv[k])
                work[end:1024, begin:end] = factors
                last = 1408 if k >= LATE else 1024
                for start in range(end, last, 256):
                    stop = min(start + 256, last)
                    work[end:1024, start:stop] -= bulk(factors, work[begin:end, start:stop])

        for hop in range(1, 5):

            @pl.when(j == 2 * hop - 1)
            def _(hop=hop):
                low_hop(hop)

    @pl.loop(0, 6)
    def _(i):
        here = pl.ds(pl.multiple_of(i * BS, BS), BS)
        block_row = 8 * (i // 2 + 1) + 2 * row + lax.rem(i, 2)
        for j in range(8):
            low[here, j * BS : (j + 1) * BS] = lraw[j, here, :] * filled(block_row, j)

    for m in range(4):
        first, second = inv[2 * m], inv[2 * m + 1]
        between = work[256 * m : 256 * m + BS, 256 * m + BS : 256 * m + 256]
        pairs[m, 0:BS, 0:BS] = first
        pairs[m, BS:256, BS:256] = second
        pairs[m, BS:256, 0:BS] = jnp.zeros((BS, BS), jnp.float32)
        pairs[m, 0:BS, BS:256] = -bulk(first, bulk(between, second))
    up_high[...], up_low[...] = halves(work[:, 1024:1408])

    for m in range(4):
        begin, end = 256 * m, 256 * m + 256
        pair = halves(pairs[m])
        above = halves(work[:begin, begin:end]) if m else None
        for a in range(3):
            here = slice(256 * a, 256 * a + 256)
            value = low[here, begin:end]
            if m:
                value = value - passes((low_high[here, :begin], low_low[here, :begin]), above)
            value = passes(halves(value), pair)
            low[here, begin:end] = value
            low_high[here, begin:end], low_low[here, begin:end] = halves(value)

    for copy in trailing:
        copy.wait()
    for a in range(3):
        here = slice(256 * a, 256 * a + 256)
        term = passes((low_high[here, :], low_low[here, :]), (up_high[...], up_low[...]))
        for h in range(2):
            for b in range(3):
                block = rest[a, b, BS * h : BS * (h + 1), :]
                block = block * filled(8 * (a + 1) + 2 * row + h, 8 * (b + 1) + col)
                block = block - term[BS * h : BS * (h + 1), BS * b : BS * (b + 1)]
                tail[a, BS * h : BS * (h + 1), BS * b : BS * (b + 1)] = block
        for d in range(1, layers):
            other = lax.rem(layer + d, layers)
            go(remote(
                tail.at[a, pl.ds(pl.multiple_of(other * 32, 32), 32), :], got.at[d, a],
                sum_send.at[d, a], sum_recv.at[d, a], other, row, col,
            ))

    mine, there = pl.ds(pl.multiple_of(row * 256, 256), 256), pl.ds(pl.multiple_of(col * BS, BS), BS)
    out_ref[pl.ds(0, 256, stride=4), :] = work[mine, there]
    for b in range(3):
        out_ref[pl.ds(b + 1, 256, stride=4), :] = work[mine, 1024 + BS * b : 1024 + BS * (b + 1)]
    for a in range(3):
        base = 1024 * (a + 1)
        out_ref[pl.ds(base, 256, stride=4), :] = low[256 * a : 256 * (a + 1), there]
        for b in range(3):
            out_ref[pl.ds(base + b + 1, 256, stride=4), :] = tail[a, :, BS * b : BS * (b + 1)]

    ours = pl.ds(pl.multiple_of(layer * 32, 32), 32)
    for a in range(3):
        for d in range(1, layers):
            place = got.at[d, a]
            remote(place, place, sum_send.at[d, a], sum_recv.at[d, a], layer, row, col).wait_recv()
        total = tail[a, ours, :]
        for d in range(1, layers):
            total = total + got[d, a]
        for b in range(3):
            anc_ref[a, b] = total[:, BS * b : BS * (b + 1)]

    for copy in sent:
        copy.wait_send()
    remote(blocks, blocks, up_send.at[2], up_recv.at[2], layer, mate, col).wait_send()
    for kind in range(2):
        for way in range(2):
            for hop in range(1, limit[kind][way]):
                place = low_part(kind, col)
                remote(
                    place, place, lo_send.at[kind, way, hop], lo_recv.at[kind, way, hop],
                    layer, row, step_to[way],
                ).wait_send()


def on_device(front_blocks, fill_mask):
    dma = pltpu.SemaphoreType.DMA
    vmem = lambda *shape: pltpu.VMEM(shape, jnp.float32)
    narrow = lambda *shape: pltpu.VMEM(shape, jnp.bfloat16)
    factored, ancestor = pl.pallas_call(
        kernel,
        out_shape=(
            jax.ShapeDtypeStruct((4096, 128), jnp.float32),
            jax.ShapeDtypeStruct((3, 3, 32, 128), jnp.float32),
        ),
        in_specs=[pl.BlockSpec(memory_space=pl.ANY), pl.BlockSpec(memory_space=pltpu.SMEM)],
        out_specs=(pl.BlockSpec(memory_space=pltpu.VMEM), pl.BlockSpec(memory_space=pltpu.VMEM)),
        scratch_shapes=[
            vmem(4, 8, 256, 128), vmem(4, 3, 256, 128), vmem(8, 768, 128),
            vmem(3, 3, 256, 128), vmem(1024, 1408), vmem(768, 1024), narrow(768, 1024), narrow(768, 1024),
            narrow(1024, 384), narrow(1024, 384), vmem(4, 256, 256), vmem(3, 256, 384), vmem(8, 3, 32, 384),
            vmem(8, 128, 128), vmem(128, 128), vmem(128, 128),
            dma((2, 2, 4)), dma((2, 2, 4)), dma((6,)), dma((2, 2, 2, 4)),
            dma((3,)), dma((3,)), dma((2, 2, 4)), dma((2, 2, 4)), dma((8, 3)), dma((8, 3)), dma((16,)),
        ],
        compiler_params=pltpu.CompilerParams(
            collective_id=0, has_side_effects=True, vmem_limit_bytes=60 * 1024 * 1024
        ),
        name="eliminate",
    )(front_blocks[0], fill_mask)
    return factored.reshape(1, 4, 256, 4, 128), ancestor.transpose(0, 2, 1, 3).reshape(3, 1, 1, 32, 3, 128)


def solution(mesh):
    split = P("layer", None, "prow", None, "pcol")
    return jax.shard_map(
        on_device,
        mesh=mesh,
        in_specs=(split, P()),
        out_specs=(split, P(None, "prow", "layer", None, None, "pcol")),
        check_vma=False,
    )
```

```python
import jax
import jax.numpy as jnp
from jax import lax
from jax.experimental import pallas as pl
from jax.experimental.pallas import tpu as pltpu
from jax.sharding import PartitionSpec as P

BS = 128
WIDE = 16
SPAN = 32
LATE = 1
MESH = pl.DeviceIdType.MESH
ORDER = (
    (0, 0, 1), (0, 1, 1), (1, 0, 0), (0, 0, 2), (0, 1, 2), (1, 1, 0), (1, 0, 1), (0, 0, 3), (0, 1, 3), (1, 1, 1),
    (1, 0, 2), (0, 0, 4), (0, 1, 4), (1, 1, 2), (1, 0, 3), (1, 1, 3), (1, 0, 4), (1, 1, 4),
)


def dot(left, right, dims=((1,), (0,)), precision=lax.Precision.HIGHEST):
    return lax.dot_general(
        left, right, (dims, ((), ())), precision=precision, preferred_element_type=jnp.float32
    )


def bulk(left, right):
    return dot(left, right, precision=lax.Precision.HIGH)


def lanes_of(block, column):
    return jnp.broadcast_to(block[:, column : column + 1], (WIDE, BS))


def row_of(block, row):
    return jnp.broadcast_to(block[row : row + 1, :], (WIDE, BS))


def invert(pivot, unit_ref, scaled_ref):
    gram = dot(pivot, pivot, ((1,), (1,)))
    count, span = BS // WIDE, SPAN // WIDE
    groups = [gram[WIDE * p : WIDE * (p + 1), :] for p in range(count)]
    lane = lax.broadcasted_iota(jnp.int32, (WIDE, BS), 1)
    sub = lax.broadcasted_iota(jnp.int32, (WIDE, BS), 0)
    raw, done = [], []
    for p in range(count):
        start, stop = WIDE * p, WIDE * (p + 1)
        if p and p % span == 0:
            term = dot(jnp.concatenate(raw, 0), jnp.concatenate(done, 0), ((0,), (0,)))
            raw, done = [], []
            for q in range(p, count):
                kept = jnp.where((lane >= start - SPAN) & (lane < start), 0.0, groups[q])
                groups[q] = kept - term[WIDE * q : WIDE * (q + 1), :]
        rows = groups[p]
        raw.append(rows)
        own = (lane >= start) & (lane < stop)
        eye = jnp.where(lane - start == sub, 1.0, 0.0)
        columns = [lanes_of(rows, start + j) for j in range(WIDE)]
        unit_ref[start:stop, :] = jnp.where(lane < start, rows, eye)
        rows = jnp.where(own, eye, rows)
        for k in range(0, WIDE, 2):
            first, second = columns[k], columns[k + 1]
            a, b = row_of(first, k), row_of(second, k)
            c, d = row_of(first, k + 1), row_of(second, k + 1)
            scale = 1.0 / (a * d - b * c)
            at, after = sub == k, sub == k + 1
            left = jnp.where(at, -d, jnp.where(after, c, first * d - second * c))
            right = jnp.where(at, b, jnp.where(after, -a, second * a - first * b))

            def cleared(block, k=k, pair=at | after, left=left, right=right, scale=scale):
                term = left * row_of(block, k) + right * row_of(block, k + 1)
                return jnp.where(pair, 0.0, block) - term * scale

            rows = cleared(rows)
            for j in range(k + 2, WIDE):
                columns[j] = cleared(columns[j])
        end = (p // span + 1) * span
        done.append(jnp.where((lane < stop) | (lane >= WIDE * end), rows, 0.0))
        scaled_ref[start:stop, :] = jnp.where(lane < stop, rows, 0.0)
        tops = [row_of(rows, k) for k in range(WIDE)]
        for q in range(p + 1, end):
            terms = [lanes_of(groups[q], start + k) * tops[k] for k in range(WIDE)]
            while len(terms) > 1:
                terms = [terms[i] + terms[i + 1] for i in range(0, len(terms), 2)]
            groups[q] = jnp.where(own, 0.0, groups[q]) - terms[0]
    right = dot(unit_ref[...], pivot)
    return dot(right, scaled_ref[...], ((0,), (0,)))


def halves(value):
    high = value.astype(jnp.bfloat16)
    return high, (value - high.astype(jnp.float32)).astype(jnp.bfloat16)


def passes(left, right):
    def one(a, b):
        return jnp.dot(a, b, preferred_element_type=jnp.float32)

    return one(left[0], right[0]) + (one(left[0], right[1]) + one(left[1], right[0]))


def kernel(
    x_ref, mask_ref, out_ref, anc_ref,
    praw, uraw, lraw, rest, work, low, low_high, low_low, up_high, up_low, pairs, tail, got, inv, unit, scaled,
    send, recv, near, far, up_send, up_recv, lo_send, lo_recv, sum_send, sum_recv, local,
):
    layer, row, col = lax.axis_index("layer"), lax.axis_index("prow"), lax.axis_index("pcol")
    cols, rows_n, layers = 8, 4, 8
    mate = row + 1 - 2 * lax.rem(row, 2)
    over = lax.rem(row + 2, rows_n)
    right, left = lax.rem(col + 1, cols), lax.rem(col + cols - 1, cols)

    first = pltpu.make_async_copy(x_ref.at[0, :, 0, :], praw.at[row, col], local.at[0])
    ups, lows = [], []
    for a in range(3):
        ups.append(pltpu.make_async_copy(x_ref.at[0, :, a + 1, :], uraw.at[row, a], local.at[4 + a]))
        lows.append(pltpu.make_async_copy(x_ref.at[a + 1, :, 0, :], lraw.at[col, pl.ds(256 * a, 256), :], local.at[1 + a]))
    trailing = [
        pltpu.make_async_copy(x_ref.at[a + 1, :, b + 1, :], rest.at[a, b], local.at[7 + 3 * a + b])
        for a in range(3)
        for b in range(3)
    ]
    first.start()
    for copy in ups:
        copy.start()

    barrier = pltpu.get_barrier_semaphore()

    def greet(*device):
        pl.semaphore_signal(barrier, inc=1, device_id=device, device_id_type=MESH)

    greet(layer, mate, col)
    greet(layer, over, col)
    greet(layer, row, right)
    greet(layer, row, left)
    for d in range(1, layers):
        greet(lax.rem(layer + d, layers), row, col)
    pl.semaphore_wait(barrier, 4 + layers - 1)

    first.wait()

    def remote(src, dst, send_sem, recv_sem, *device):
        return pltpu.make_async_remote_copy(
            src_ref=src, dst_ref=dst, send_sem=send_sem, recv_sem=recv_sem,
            device_id=device, device_id_type=MESH,
        )

    sent = []

    def go(copy):
        copy.start()
        sent.append(copy)

    groups = (row, over)
    limit = ((4, 3), (3, 4))
    step_to = (right, left)

    def origin(way, hop):
        return lax.rem(col + (cols - hop if way == 0 else hop), cols)

    def chunk_at(group, source, chunk):
        return praw.at[group, source, pl.ds(BS * chunk, BS), :]

    def ring(place, kind, chunk, way, hop):
        return remote(
            place, place, send.at[kind, chunk, way, hop], recv.at[kind, chunk, way, hop], layer, row, step_to[way]
        )

    def passed(place, kind, chunk, way, hop):
        return remote(
            place, place, far.at[0, kind, chunk, way, hop], far.at[1, kind, chunk, way, hop], layer, mate, col
        )

    def across(place, chunk):
        return remote(place, place, near.at[0, chunk], near.at[1, chunk], layer, over, col)

    def beside(place, kind, chunk):
        return remote(place, place, near.at[2 + 2 * kind, chunk], near.at[3 + 2 * kind, chunk], layer, mate, col)

    for chunk in range(2):
        place = chunk_at(row, col, chunk)
        go(across(place, chunk))
        for way in range(2):
            go(ring(place, 0, chunk, way, 0))
    for copy in lows + trailing:
        copy.start()
    for chunk in range(2):
        go(beside(chunk_at(row, col, chunk), 0, chunk))
    for copy in ups:
        copy.wait()
    blocks = uraw.at[row]
    go(remote(blocks, blocks, up_send.at[0], up_recv.at[0], layer, over, col))

    for kind, chunk, hop in ORDER:
        if hop == 0:
            place = chunk_at(over, col, chunk)
            across(place, chunk).wait_recv()
            for way in range(2):
                go(ring(place, 1, chunk, way, 0))
            go(beside(place, 1, chunk))
            continue
        for way in range(2):
            if hop > limit[chunk][way]:
                continue
            place = chunk_at(groups[kind], origin(way, hop), chunk)
            ring(place, kind, chunk, way, hop - 1).wait_recv()
            if hop < limit[chunk][way]:
                go(ring(place, kind, chunk, way, hop))
            go(passed(place, kind, chunk, way, hop - 1))

    def low_part(kind, source):
        return lraw.at[source, pl.ds(384 * kind, 384), :]

    for copy in lows:
        copy.wait()
    for kind in range(2):
        for way in range(2):
            half = low_part(kind, col)
            go(remote(
                half, half, lo_send.at[kind, way, 0], lo_recv.at[kind, way, 0],
                layer, row, step_to[way],
            ))

    def low_ring(place, kind, way, hop):
        return remote(
            place, place, lo_send.at[kind, way, hop], lo_recv.at[kind, way, hop], layer, row, step_to[way]
        )

    def low_hop(kind, hop):
        for way in range(2):
            if hop > limit[kind][way]:
                continue
            place = low_part(kind, origin(way, hop))
            low_ring(place, kind, way, hop - 1).wait_recv()
            if hop < limit[kind][way]:
                low_ring(place, kind, way, hop).start()

    go(remote(blocks, blocks, up_send.at[1], up_recv.at[1], layer, mate, col))

    mates = (mate, rows_n - 1 - row)
    for kind, chunk, hop in ORDER:
        if hop == 0:
            beside(chunk_at(mates[1], col, chunk), 1, chunk).wait_recv()
            beside(chunk_at(mates[0], col, chunk), 0, chunk).wait_recv()
            continue
        for way in range(2):
            if hop <= limit[chunk][way]:
                place = chunk_at(mates[kind], origin(way, hop), chunk)
                passed(place, kind, chunk, way, hop - 1).wait_recv()

    def up_over():
        place = uraw.at[over]
        remote(place, place, up_send.at[0], up_recv.at[0], layer, over, col).wait_recv()
        remote(place, place, up_send.at[2], up_recv.at[2], layer, mate, col).start()

    def up_here():
        for k in range(2):
            place = uraw.at[mates[k]]
            remote(place, place, up_send.at[1 + k], up_recv.at[1 + k], layer, mate, col).wait_recv()
        for i in range(8):
            for b in range(3):
                work[i * BS : (i + 1) * BS, 1024 + b * BS : 1024 + (b + 1) * BS] = (
                    uraw[i // 2, b, (i % 2) * BS : (i % 2 + 1) * BS, :] * filled(i, 8 * (b + 1) + col)
                )
        for k in range(LATE):
            begin, end = k * BS, (k + 1) * BS
            work[end:1024, 1024:1408] -= bulk(work[end:1024, begin:end], work[begin:end, 1024:1408])

    def filled(i, j):
        return mask_ref[i, j].astype(jnp.float32)

    @pl.loop(0, 8)
    def _(i):
        group, part = i // 2, pl.multiple_of(lax.rem(i, 2) * BS, BS)
        here = pl.ds(pl.multiple_of(i * BS, BS), BS)
        for j in range(8):
            work[here, j * BS : (j + 1) * BS] = praw[group, j, pl.ds(part, BS), :] * filled(i, j)

    @pl.loop(0, 8)
    def _(j):
        here = pl.ds(pl.multiple_of(j * BS, BS), BS)
        inv[j] = invert(work[here, here], unit, scaled)
        pl.when(j == 0)(up_over)
        pl.when(j == LATE)(up_here)
        for k in range(7):

            @pl.when(j == k)
            def _(k=k):
                begin, end = k * BS, (k + 1) * BS
                factors = bulk(work[end:1024, begin:end], inv[k])
                work[end:1024, begin:end] = factors
                last = 1408 if k >= LATE else 1024
                for start in range(end, last, 256):
                    stop = min(start + 256, last)
                    work[end:1024, start:stop] -= bulk(factors, work[begin:end, start:stop])

        for hop in range(1, 5):
            for kind in range(2):

                @pl.when(j == 2 * hop - 2 + kind)
                def _(kind=kind, hop=hop):
                    low_hop(kind, hop)

    @pl.loop(0, 6)
    def _(i):
        here = pl.ds(pl.multiple_of(i * BS, BS), BS)
        block_row = 8 * (i // 2 + 1) + 2 * row + lax.rem(i, 2)
        for j in range(8):
            low[here, j * BS : (j + 1) * BS] = lraw[j, here, :] * filled(block_row, j)

    for m in range(4):
        first, second = inv[2 * m], inv[2 * m + 1]
        between = work[256 * m : 256 * m + BS, 256 * m + BS : 256 * m + 256]
        pairs[m, 0:BS, 0:BS] = first
        pairs[m, BS:256, BS:256] = second
        pairs[m, BS:256, 0:BS] = jnp.zeros((BS, BS), jnp.float32)
        pairs[m, 0:BS, BS:256] = -bulk(first, bulk(between, second))
    up_high[...], up_low[...] = halves(work[:, 1024:1408])

    for m in range(4):
        begin, end = 256 * m, 256 * m + 256
        pair = halves(pairs[m])
        above = halves(work[:begin, begin:end]) if m else None
        for a in range(3):
            here = slice(256 * a, 256 * a + 256)
            value = low[here, begin:end]
            if m:
                value = value - passes((low_high[here, :begin], low_low[here, :begin]), above)
            value = passes(halves(value), pair)
            low[here, begin:end] = value
            low_high[here, begin:end], low_low[here, begin:end] = halves(value)

    for copy in trailing:
        copy.wait()
    for a in range(3):
        here = slice(256 * a, 256 * a + 256)
        term = passes((low_high[here, :], low_low[here, :]), (up_high[...], up_low[...]))
        for h in range(2):
            for b in range(3):
                block = rest[a, b, BS * h : BS * (h + 1), :]
                block = block * filled(8 * (a + 1) + 2 * row + h, 8 * (b + 1) + col)
                block = block - term[BS * h : BS * (h + 1), BS * b : BS * (b + 1)]
                tail[a, BS * h : BS * (h + 1), BS * b : BS * (b + 1)] = block
        for d in range(1, layers):
            other = lax.rem(layer + d, layers)
            go(remote(
                tail.at[a, pl.ds(pl.multiple_of(other * 32, 32), 32), :], got.at[d, a],
                sum_send.at[d, a], sum_recv.at[d, a], other, row, col,
            ))

    mine, there = pl.ds(pl.multiple_of(row * 256, 256), 256), pl.ds(pl.multiple_of(col * BS, BS), BS)
    out_ref[pl.ds(0, 256, stride=4), :] = work[mine, there]
    for b in range(3):
        out_ref[pl.ds(b + 1, 256, stride=4), :] = work[mine, 1024 + BS * b : 1024 + BS * (b + 1)]
    for a in range(3):
        base = 1024 * (a + 1)
        out_ref[pl.ds(base, 256, stride=4), :] = low[256 * a : 256 * (a + 1), there]
        for b in range(3):
            out_ref[pl.ds(base + b + 1, 256, stride=4), :] = tail[a, :, BS * b : BS * (b + 1)]

    ours = pl.ds(pl.multiple_of(layer * 32, 32), 32)
    for a in range(3):
        for d in range(1, layers):
            place = got.at[d, a]
            remote(place, place, sum_send.at[d, a], sum_recv.at[d, a], layer, row, col).wait_recv()
        total = tail[a, ours, :]
        for d in range(1, layers):
            total = total + got[d, a]
        for b in range(3):
            anc_ref[a, b] = total[:, BS * b : BS * (b + 1)]

    for copy in sent:
        copy.wait_send()
    remote(blocks, blocks, up_send.at[2], up_recv.at[2], layer, mate, col).wait_send()
    for kind in range(2):
        for way in range(2):
            for hop in range(1, limit[kind][way]):
                low_ring(low_part(kind, col), kind, way, hop).wait_send()


def handed_on(staged_ref, out_ref, sems):
    copies = [
        pltpu.make_async_copy(staged_ref.at[pl.ds(1024 * k, 1024)], out_ref.at[pl.ds(1024 * k, 1024)], sems.at[k])
        for k in range(4)
    ]
    for copy in copies:
        copy.start()
    for copy in copies:
        copy.wait()


def on_device(front_blocks, fill_mask):
    dma = pltpu.SemaphoreType.DMA
    vmem = lambda *shape: pltpu.VMEM(shape, jnp.float32)
    narrow = lambda *shape: pltpu.VMEM(shape, jnp.bfloat16)
    factored, ancestor = pl.pallas_call(
        kernel,
        out_shape=(
            pltpu.VMEM((4096, 128), jnp.float32),
            jax.ShapeDtypeStruct((3, 3, 32, 128), jnp.float32),
        ),
        in_specs=[pl.BlockSpec(memory_space=pl.ANY), pl.BlockSpec(memory_space=pltpu.SMEM)],
        out_specs=(pl.BlockSpec(memory_space=pltpu.VMEM), pl.BlockSpec(memory_space=pltpu.VMEM)),
        scratch_shapes=[
            vmem(4, 8, 256, 128), vmem(4, 3, 256, 128), vmem(8, 768, 128),
            vmem(3, 3, 256, 128), vmem(1024, 1408), vmem(768, 1024), narrow(768, 1024), narrow(768, 1024),
            narrow(1024, 384), narrow(1024, 384), vmem(4, 256, 256), vmem(3, 256, 384), vmem(8, 3, 32, 384),
            vmem(8, 128, 128), vmem(128, 128), vmem(128, 128),
            dma((2, 2, 2, 4)), dma((2, 2, 2, 4)), dma((6, 2)), dma((2, 2, 2, 2, 4)),
            dma((3,)), dma((3,)), dma((2, 2, 4)), dma((2, 2, 4)), dma((8, 3)), dma((8, 3)), dma((16,)),
        ],
        compiler_params=pltpu.CompilerParams(
            collective_id=0, has_side_effects=True, vmem_limit_bytes=60 * 1024 * 1024
        ),
        name="eliminate",
    )(front_blocks[0], fill_mask)
    factored = pl.pallas_call(
        handed_on, out_shape=jax.ShapeDtypeStruct((4096, 128), jnp.float32),
        in_specs=[pl.BlockSpec(memory_space=pltpu.VMEM)], out_specs=pl.BlockSpec(memory_space=pl.ANY),
        scratch_shapes=[dma((4,))], name="hand_on",
    )(pltpu.with_memory_space_constraint(factored, pltpu.VMEM))
    return factored.reshape(1, 4, 256, 4, 128), ancestor.transpose(0, 2, 1, 3).reshape(3, 1, 1, 32, 3, 128)


def solution(mesh):
    split = P("layer", None, "prow", None, "pcol")
    return jax.shard_map(
        on_device,
        mesh=mesh,
        in_specs=(split, P()),
        out_specs=(split, P(None, "prow", "layer", None, None, "pcol")),
        check_vma=False,
    )
```

```python
import jax
import jax.numpy as jnp
from jax import lax
from jax.experimental import pallas as pl
from jax.experimental.pallas import tpu as pltpu
from jax.sharding import PartitionSpec as P

BS = 128
WIDE = 16
SPAN = 32
LATE = 1
MESH = pl.DeviceIdType.MESH
ORDER = (
    (0, 0, 1), (0, 1, 1), (1, 0, 0), (0, 0, 2), (0, 1, 2), (1, 1, 0), (1, 0, 1), (0, 0, 3), (0, 1, 3), (1, 1, 1),
    (1, 0, 2), (0, 0, 4), (0, 1, 4), (1, 1, 2), (1, 0, 3), (1, 1, 3), (1, 0, 4), (1, 1, 4),
)


def dot(left, right, dims=((1,), (0,)), precision=lax.Precision.HIGHEST):
    return lax.dot_general(
        left, right, (dims, ((), ())), precision=precision, preferred_element_type=jnp.float32
    )


def bulk(left, right):
    return dot(left, right, precision=lax.Precision.HIGH)


def lanes_of(block, column):
    return jnp.broadcast_to(block[:, column : column + 1], (WIDE, BS))


def row_of(block, row):
    return jnp.broadcast_to(block[row : row + 1, :], (WIDE, BS))


def invert(pivot, unit_ref, scaled_ref):
    gram = dot(pivot, pivot, ((1,), (1,)))
    count, span = BS // WIDE, SPAN // WIDE
    groups = [gram[WIDE * p : WIDE * (p + 1), :] for p in range(count)]
    lane = lax.broadcasted_iota(jnp.int32, (WIDE, BS), 1)
    sub = lax.broadcasted_iota(jnp.int32, (WIDE, BS), 0)
    raw, done = [], []
    for p in range(count):
        start, stop = WIDE * p, WIDE * (p + 1)
        if p and p % span == 0:
            term = dot(jnp.concatenate(raw, 0), jnp.concatenate(done, 0), ((0,), (0,)))
            raw, done = [], []
            for q in range(p, count):
                kept = jnp.where((lane >= start - SPAN) & (lane < start), 0.0, groups[q])
                groups[q] = kept - term[WIDE * q : WIDE * (q + 1), :]
        rows = groups[p]
        raw.append(rows)
        own = (lane >= start) & (lane < stop)
        eye = jnp.where(lane - start == sub, 1.0, 0.0)
        columns = [lanes_of(rows, start + j) for j in range(WIDE)]
        unit_ref[start:stop, :] = jnp.where(lane < start, rows, eye)
        rows = jnp.where(own, eye, rows)
        for k in range(0, WIDE, 2):
            first, second = columns[k], columns[k + 1]
            a, b = row_of(first, k), row_of(second, k)
            c, d = row_of(first, k + 1), row_of(second, k + 1)
            scale = 1.0 / (a * d - b * c)
            at, after = sub == k, sub == k + 1
            left = jnp.where(at, -d, jnp.where(after, c, first * d - second * c))
            right = jnp.where(at, b, jnp.where(after, -a, second * a - first * b))

            def cleared(block, k=k, pair=at | after, left=left, right=right, scale=scale):
                term = left * row_of(block, k) + right * row_of(block, k + 1)
                return jnp.where(pair, 0.0, block) - term * scale

            rows = cleared(rows)
            for j in range(k + 2, WIDE):
                columns[j] = cleared(columns[j])
        end = (p // span + 1) * span
        done.append(jnp.where((lane < stop) | (lane >= WIDE * end), rows, 0.0))
        scaled_ref[start:stop, :] = jnp.where(lane < stop, rows, 0.0)
        tops = [row_of(rows, k) for k in range(WIDE)]
        for q in range(p + 1, end):
            terms = [lanes_of(groups[q], start + k) * tops[k] for k in range(WIDE)]
            while len(terms) > 1:
                terms = [terms[i] + terms[i + 1] for i in range(0, len(terms), 2)]
            groups[q] = jnp.where(own, 0.0, groups[q]) - terms[0]
    right = dot(unit_ref[...], pivot)
    return dot(right, scaled_ref[...], ((0,), (0,)))


def halves(value):
    high = value.astype(jnp.bfloat16)
    return high, (value - high.astype(jnp.float32)).astype(jnp.bfloat16)


def passes(left, right):
    def one(a, b):
        return jnp.dot(a, b, preferred_element_type=jnp.float32)

    return one(left[0], right[0]) + (one(left[0], right[1]) + one(left[1], right[0]))


def kernel(
    x_ref, mask_ref, out_ref, anc_ref,
    praw, uraw, lraw, rest, work, low, low_high, low_low, up_high, up_low, pairs, tail, got, inv, unit, scaled,
    send, recv, near, far, up_send, up_recv, lo_send, lo_recv, sum_send, sum_recv, local,
):
    layer, row, col = lax.axis_index("layer"), lax.axis_index("prow"), lax.axis_index("pcol")
    cols, rows_n, layers = 8, 4, 8
    mate = row + 1 - 2 * lax.rem(row, 2)
    over = lax.rem(row + 2, rows_n)
    right, left = lax.rem(col + 1, cols), lax.rem(col + cols - 1, cols)

    first = pltpu.make_async_copy(x_ref.at[0, :, 0, :], praw.at[row, col], local.at[0])
    ups, lows = [], []
    for a in range(3):
        ups.append(pltpu.make_async_copy(x_ref.at[0, :, a + 1, :], uraw.at[row, a], local.at[4 + a]))
        lows.append(pltpu.make_async_copy(x_ref.at[a + 1, :, 0, :], lraw.at[col, pl.ds(256 * a, 256), :], local.at[1 + a]))
    trailing = [
        pltpu.make_async_copy(x_ref.at[a + 1, :, b + 1, :], rest.at[a, b], local.at[7 + 3 * a + b])
        for a in range(3)
        for b in range(3)
    ]
    first.start()
    for copy in ups:
        copy.start()

    barrier = pltpu.get_barrier_semaphore()

    def greet(*device):
        pl.semaphore_signal(barrier, inc=1, device_id=device, device_id_type=MESH)

    greet(layer, mate, col)
    greet(layer, over, col)
    greet(layer, row, right)
    greet(layer, row, left)
    for d in range(1, layers):
        greet(lax.rem(layer + d, layers), row, col)
    pl.semaphore_wait(barrier, 4 + layers - 1)

    first.wait()

    def remote(src, dst, send_sem, recv_sem, *device):
        return pltpu.make_async_remote_copy(
            src_ref=src, dst_ref=dst, send_sem=send_sem, recv_sem=recv_sem,
            device_id=device, device_id_type=MESH,
        )

    sent = []

    def go(copy):
        copy.start()
        sent.append(copy)

    groups = (row, over)
    limit = ((4, 3), (3, 4))
    step_to = (right, left)

    def origin(way, hop):
        return lax.rem(col + (cols - hop if way == 0 else hop), cols)

    def chunk_at(group, source, chunk):
        return praw.at[group, source, pl.ds(BS * chunk, BS), :]

    def ring(place, kind, chunk, way, hop):
        return remote(
            place, place, send.at[kind, chunk, way, hop], recv.at[kind, chunk, way, hop], layer, row, step_to[way]
        )

    def passed(place, kind, chunk, way, hop):
        return remote(
            place, place, far.at[0, kind, chunk, way, hop], far.at[1, kind, chunk, way, hop], layer, mate, col
        )

    def across(place, chunk):
        return remote(place, place, near.at[0, chunk], near.at[1, chunk], layer, over, col)

    def beside(place, kind, chunk):
        return remote(place, place, near.at[2 + 2 * kind, chunk], near.at[3 + 2 * kind, chunk], layer, mate, col)

    for chunk in range(2):
        place = chunk_at(row, col, chunk)
        go(across(place, chunk))
        for way in range(2):
            go(ring(place, 0, chunk, way, 0))
    for copy in lows + trailing:
        copy.start()
    for chunk in range(2):
        go(beside(chunk_at(row, col, chunk), 0, chunk))
    for copy in ups:
        copy.wait()
    blocks = uraw.at[row]
    go(remote(blocks, blocks, up_send.at[0], up_recv.at[0], layer, over, col))

    for kind, chunk, hop in ORDER:
        if hop == 0:
            place = chunk_at(over, col, chunk)
            across(place, chunk).wait_recv()
            for way in range(2):
                go(ring(place, 1, chunk, way, 0))
            go(beside(place, 1, chunk))
            continue
        for way in range(2):
            if hop > limit[chunk][way]:
                continue
            place = chunk_at(groups[kind], origin(way, hop), chunk)
            ring(place, kind, chunk, way, hop - 1).wait_recv()
            if hop < limit[chunk][way]:
                go(ring(place, kind, chunk, way, hop))
            go(passed(place, kind, chunk, way, hop - 1))

    def low_part(kind, source):
        return lraw.at[source, pl.ds(384 * kind, 384), :]

    for copy in lows:
        copy.wait()
    for kind in range(2):
        for way in range(2):
            half = low_part(kind, col)
            go(remote(
                half, half, lo_send.at[kind, way, 0], lo_recv.at[kind, way, 0],
                layer, row, step_to[way],
            ))

    def low_ring(place, kind, way, hop):
        return remote(
            place, place, lo_send.at[kind, way, hop], lo_recv.at[kind, way, hop], layer, row, step_to[way]
        )

    def low_hop(kind, hop):
        for way in range(2):
            if hop > limit[kind][way]:
                continue
            place = low_part(kind, origin(way, hop))
            low_ring(place, kind, way, hop - 1).wait_recv()
            if hop < limit[kind][way]:
                low_ring(place, kind, way, hop).start()

    go(remote(blocks, blocks, up_send.at[1], up_recv.at[1], layer, mate, col))

    mates = (mate, rows_n - 1 - row)
    for kind, chunk, hop in ORDER:
        if hop == 0:
            beside(chunk_at(mates[1], col, chunk), 1, chunk).wait_recv()
            beside(chunk_at(mates[0], col, chunk), 0, chunk).wait_recv()
            continue
        for way in range(2):
            if hop <= limit[chunk][way]:
                place = chunk_at(mates[kind], origin(way, hop), chunk)
                passed(place, kind, chunk, way, hop - 1).wait_recv()

    def up_over():
        place = uraw.at[over]
        remote(place, place, up_send.at[0], up_recv.at[0], layer, over, col).wait_recv()
        remote(place, place, up_send.at[2], up_recv.at[2], layer, mate, col).start()

    def up_here():
        for k in range(2):
            place = uraw.at[mates[k]]
            remote(place, place, up_send.at[1 + k], up_recv.at[1 + k], layer, mate, col).wait_recv()
        for i in range(8):
            for b in range(3):
                work[i * BS : (i + 1) * BS, 1024 + b * BS : 1024 + (b + 1) * BS] = (
                    uraw[i // 2, b, (i % 2) * BS : (i % 2 + 1) * BS, :] * filled(i, 8 * (b + 1) + col)
                )
        for k in range(LATE):
            begin, end = k * BS, (k + 1) * BS
            work[end:1024, 1024:1408] -= bulk(work[end:1024, begin:end], work[begin:end, 1024:1408])

    def filled(i, j):
        return mask_ref[i, j].astype(jnp.float32)

    @pl.loop(0, 8)
    def _(i):
        group, part = i // 2, pl.multiple_of(lax.rem(i, 2) * BS, BS)
        here = pl.ds(pl.multiple_of(i * BS, BS), BS)
        for j in range(8):
            work[here, j * BS : (j + 1) * BS] = praw[group, j, pl.ds(part, BS), :] * filled(i, j)

    @pl.loop(0, 8)
    def _(j):
        here = pl.ds(pl.multiple_of(j * BS, BS), BS)
        inv[j] = invert(work[here, here], unit, scaled)
        pl.when(j == 0)(up_over)
        pl.when(j == LATE)(up_here)
        for k in range(7):

            @pl.when(j == k)
            def _(k=k):
                begin, end = k * BS, (k + 1) * BS
                factors = bulk(work[end:1024, begin:end], inv[k])
                work[end:1024, begin:end] = factors
                last = 1408 if k >= LATE else 1024
                for start in range(end, last, 256):
                    stop = min(start + 256, last)
                    work[end:1024, start:stop] -= bulk(factors, work[begin:end, start:stop])

        for hop in range(1, 5):
            for kind in range(2 if hop < 4 else 1):

                @pl.when(j == 2 * hop - 2 + kind)
                def _(kind=kind, hop=hop):
                    low_hop(kind, hop)

    for m in range(4):
        first, second = inv[2 * m], inv[2 * m + 1]
        between = work[256 * m : 256 * m + BS, 256 * m + BS : 256 * m + 256]
        pairs[m, 0:BS, 0:BS] = first
        pairs[m, BS:256, BS:256] = second
        pairs[m, BS:256, 0:BS] = jnp.zeros((BS, BS), jnp.float32)
        pairs[m, 0:BS, BS:256] = -bulk(first, bulk(between, second))
    up_high[...], up_low[...] = halves(work[:, 1024:1408])

    def solve(supers):
        for a in supers:
            for h in range(2):
                here = slice(256 * a + BS * h, 256 * a + BS * (h + 1))
                for j in range(8):
                    low[here, j * BS : (j + 1) * BS] = lraw[j, here, :] * filled(8 * (a + 1) + 2 * row + h, j)
        for m in range(4):
            begin, end = 256 * m, 256 * m + 256
            pair = halves(pairs[m])
            above = halves(work[:begin, begin:end]) if m else None
            for a in supers:
                here = slice(256 * a, 256 * a + 256)
                value = low[here, begin:end]
                if m:
                    value = value - passes((low_high[here, :begin], low_low[here, :begin]), above)
                value = passes(halves(value), pair)
                low[here, begin:end] = value
                low_high[here, begin:end], low_low[here, begin:end] = halves(value)
        for a in supers:
            here = slice(256 * a, 256 * a + 256)
            term = passes((low_high[here, :], low_low[here, :]), (up_high[...], up_low[...]))
            for h in range(2):
                for b in range(3):
                    block = rest[a, b, BS * h : BS * (h + 1), :]
                    block = block * filled(8 * (a + 1) + 2 * row + h, 8 * (b + 1) + col)
                    block = block - term[BS * h : BS * (h + 1), BS * b : BS * (b + 1)]
                    tail[a, BS * h : BS * (h + 1), BS * b : BS * (b + 1)] = block
            for d in range(1, layers):
                other = lax.rem(layer + d, layers)
                go(remote(
                    tail.at[a, pl.ds(pl.multiple_of(other * 32, 32), 32), :], got.at[d, a],
                    sum_send.at[d, a], sum_recv.at[d, a], other, row, col,
                ))

    for copy in trailing:
        copy.wait()
    solve((0,))
    low_hop(1, 4)
    solve((1, 2))

    mine, there = pl.ds(pl.multiple_of(row * 256, 256), 256), pl.ds(pl.multiple_of(col * BS, BS), BS)
    out_ref[pl.ds(0, 256, stride=4), :] = work[mine, there]
    for b in range(3):
        out_ref[pl.ds(b + 1, 256, stride=4), :] = work[mine, 1024 + BS * b : 1024 + BS * (b + 1)]
    for a in range(3):
        base = 1024 * (a + 1)
        out_ref[pl.ds(base, 256, stride=4), :] = low[256 * a : 256 * (a + 1), there]
        for b in range(3):
            out_ref[pl.ds(base + b + 1, 256, stride=4), :] = tail[a, :, BS * b : BS * (b + 1)]

    ours = pl.ds(pl.multiple_of(layer * 32, 32), 32)
    for a in range(3):
        for d in range(1, layers):
            place = got.at[d, a]
            remote(place, place, sum_send.at[d, a], sum_recv.at[d, a], layer, row, col).wait_recv()
        total = tail[a, ours, :]
        for d in range(1, layers):
            total = total + got[d, a]
        for b in range(3):
            anc_ref[a, b] = total[:, BS * b : BS * (b + 1)]

    for copy in sent:
        copy.wait_send()
    remote(blocks, blocks, up_send.at[2], up_recv.at[2], layer, mate, col).wait_send()
    for kind in range(2):
        for way in range(2):
            for hop in range(1, limit[kind][way]):
                low_ring(low_part(kind, col), kind, way, hop).wait_send()


def handed_on(staged_ref, out_ref, sems):
    copies = [
        pltpu.make_async_copy(staged_ref.at[pl.ds(1024 * k, 1024)], out_ref.at[pl.ds(1024 * k, 1024)], sems.at[k])
        for k in range(4)
    ]
    for copy in copies:
        copy.start()
    for copy in copies:
        copy.wait()


def on_device(front_blocks, fill_mask):
    dma = pltpu.SemaphoreType.DMA
    vmem = lambda *shape: pltpu.VMEM(shape, jnp.float32)
    narrow = lambda *shape: pltpu.VMEM(shape, jnp.bfloat16)
    factored, ancestor = pl.pallas_call(
        kernel,
        out_shape=(
            pltpu.VMEM((4096, 128), jnp.float32),
            jax.ShapeDtypeStruct((3, 3, 32, 128), jnp.float32),
        ),
        in_specs=[pl.BlockSpec(memory_space=pl.ANY), pl.BlockSpec(memory_space=pltpu.SMEM)],
        out_specs=(pl.BlockSpec(memory_space=pltpu.VMEM), pl.BlockSpec(memory_space=pltpu.VMEM)),
        scratch_shapes=[
            vmem(4, 8, 256, 128), vmem(4, 3, 256, 128), vmem(8, 768, 128),
            vmem(3, 3, 256, 128), vmem(1024, 1408), vmem(768, 1024), narrow(768, 1024), narrow(768, 1024),
            narrow(1024, 384), narrow(1024, 384), vmem(4, 256, 256), vmem(3, 256, 384), vmem(8, 3, 32, 384),
            vmem(8, 128, 128), vmem(128, 128), vmem(128, 128),
            dma((2, 2, 2, 4)), dma((2, 2, 2, 4)), dma((6, 2)), dma((2, 2, 2, 2, 4)),
            dma((3,)), dma((3,)), dma((2, 2, 4)), dma((2, 2, 4)), dma((8, 3)), dma((8, 3)), dma((16,)),
        ],
        compiler_params=pltpu.CompilerParams(
            collective_id=0, has_side_effects=True, vmem_limit_bytes=60 * 1024 * 1024
        ),
        name="eliminate",
    )(front_blocks[0], fill_mask)
    factored = pl.pallas_call(
        handed_on, out_shape=jax.ShapeDtypeStruct((4096, 128), jnp.float32),
        in_specs=[pl.BlockSpec(memory_space=pltpu.VMEM)], out_specs=pl.BlockSpec(memory_space=pl.ANY),
        scratch_shapes=[dma((4,))], name="hand_on",
    )(pltpu.with_memory_space_constraint(factored, pltpu.VMEM))
    return factored.reshape(1, 4, 256, 4, 128), ancestor.transpose(0, 2, 1, 3).reshape(3, 1, 1, 32, 3, 128)


def solution(mesh):
    split = P("layer", None, "prow", None, "pcol")
    return jax.shard_map(
        on_device,
        mesh=mesh,
        in_specs=(split, P()),
        out_specs=(split, P(None, "prow", "layer", None, None, "pcol")),
        check_vma=False,
    )
```

```python
import jax
import jax.numpy as jnp
from jax import lax
from jax.experimental import pallas as pl
from jax.experimental.pallas import tpu as pltpu
from jax.sharding import PartitionSpec as P

BS = 128
WIDE = 16
SPAN = 32
LATE = 1
MESH = pl.DeviceIdType.MESH
ORDER = (
    (0, 0, 1), (0, 1, 1), (1, 0, 0), (0, 0, 2), (0, 1, 2), (1, 1, 0), (1, 0, 1), (0, 0, 3), (0, 1, 3), (1, 1, 1),
    (1, 0, 2), (0, 0, 4), (0, 1, 4), (1, 1, 2), (1, 0, 3), (1, 1, 3), (1, 0, 4), (1, 1, 4),
)


def dot(left, right, dims=((1,), (0,)), precision=lax.Precision.HIGHEST):
    return lax.dot_general(
        left, right, (dims, ((), ())), precision=precision, preferred_element_type=jnp.float32
    )


def bulk(left, right):
    return dot(left, right, precision=lax.Precision.HIGH)


def lanes_of(block, column):
    return jnp.broadcast_to(block[:, column : column + 1], (WIDE, BS))


def row_of(block, row):
    return jnp.broadcast_to(block[row : row + 1, :], (WIDE, BS))


def invert(pivot, unit_ref, scaled_ref):
    gram = dot(pivot, pivot, ((1,), (1,)))
    count, span = BS // WIDE, SPAN // WIDE
    groups = [gram[WIDE * p : WIDE * (p + 1), :] for p in range(count)]
    lane = lax.broadcasted_iota(jnp.int32, (WIDE, BS), 1)
    sub = lax.broadcasted_iota(jnp.int32, (WIDE, BS), 0)
    raw, done = [], []
    for p in range(count):
        start, stop = WIDE * p, WIDE * (p + 1)
        if p and p % span == 0:
            term = dot(jnp.concatenate(raw, 0), jnp.concatenate(done, 0), ((0,), (0,)))
            raw, done = [], []
            for q in range(p, count):
                kept = jnp.where((lane >= start - SPAN) & (lane < start), 0.0, groups[q])
                groups[q] = kept - term[WIDE * q : WIDE * (q + 1), :]
        rows = groups[p]
        raw.append(rows)
        own = (lane >= start) & (lane < stop)
        eye = jnp.where(lane - start == sub, 1.0, 0.0)
        columns = [lanes_of(rows, start + j) for j in range(WIDE)]
        unit_ref[start:stop, :] = jnp.where(lane < start, rows, eye)
        rows = jnp.where(own, eye, rows)
        for k in range(0, WIDE, 2):
            first, second = columns[k], columns[k + 1]
            a, b = row_of(first, k), row_of(second, k)
            c, d = row_of(first, k + 1), row_of(second, k + 1)
            scale = 1.0 / (a * d - b * c)
            at, after = sub == k, sub == k + 1
            left = jnp.where(at, -d, jnp.where(after, c, first * d - second * c))
            right = jnp.where(at, b, jnp.where(after, -a, second * a - first * b))

            def cleared(block, k=k, pair=at | after, left=left, right=right, scale=scale):
                term = left * row_of(block, k) + right * row_of(block, k + 1)
                return jnp.where(pair, 0.0, block) - term * scale

            rows = cleared(rows)
            for j in range(k + 2, WIDE):
                columns[j] = cleared(columns[j])
        end = (p // span + 1) * span
        done.append(jnp.where((lane < stop) | (lane >= WIDE * end), rows, 0.0))
        scaled_ref[start:stop, :] = jnp.where(lane < stop, rows, 0.0)
        tops = [row_of(rows, k) for k in range(WIDE)]
        for q in range(p + 1, end):
            terms = [lanes_of(groups[q], start + k) * tops[k] for k in range(WIDE)]
            while len(terms) > 1:
                terms = [terms[i] + terms[i + 1] for i in range(0, len(terms), 2)]
            groups[q] = jnp.where(own, 0.0, groups[q]) - terms[0]
    right = dot(unit_ref[...], pivot)
    return dot(right, scaled_ref[...], ((0,), (0,)))


def halves(value):
    high = value.astype(jnp.bfloat16)
    return high, (value - high.astype(jnp.float32)).astype(jnp.bfloat16)


def passes(left, right):
    def one(a, b):
        return jnp.dot(a, b, preferred_element_type=jnp.float32)

    return one(left[0], right[0]) + (one(left[0], right[1]) + one(left[1], right[0]))


def kernel(
    x_ref, mask_ref, out_ref, anc_ref,
    praw, uraw, lraw, rest, work, low, low_high, low_low, up_high, up_low, pairs, tail, got, inv, unit, scaled,
    send, recv, near, far, up_send, up_recv, lo_send, lo_recv, sum_send, sum_recv, local,
):
    layer, row, col = lax.axis_index("layer"), lax.axis_index("prow"), lax.axis_index("pcol")
    cols, rows_n, layers = 8, 4, 8
    mate = row + 1 - 2 * lax.rem(row, 2)
    over = lax.rem(row + 2, rows_n)
    right, left = lax.rem(col + 1, cols), lax.rem(col + cols - 1, cols)

    first = pltpu.make_async_copy(x_ref.at[0, :, 0, :], praw.at[row, col], local.at[0])
    ups, lows = [], []
    for a in range(3):
        ups.append(pltpu.make_async_copy(x_ref.at[0, :, a + 1, :], uraw.at[row, a], local.at[4 + a]))
        lows.append(pltpu.make_async_copy(x_ref.at[a + 1, :, 0, :], lraw.at[col, pl.ds(256 * a, 256), :], local.at[1 + a]))
    trailing = [
        pltpu.make_async_copy(x_ref.at[a + 1, :, b + 1, :], rest.at[a, b], local.at[7 + 3 * a + b])
        for a in range(3)
        for b in range(3)
    ]
    first.start()
    for copy in ups:
        copy.start()

    barrier = pltpu.get_barrier_semaphore()

    def greet(*device):
        pl.semaphore_signal(barrier, inc=1, device_id=device, device_id_type=MESH)

    greet(layer, mate, col)
    greet(layer, over, col)
    greet(layer, row, right)
    greet(layer, row, left)
    for d in range(1, layers):
        greet(lax.rem(layer + d, layers), row, col)
    pl.semaphore_wait(barrier, 4 + layers - 1)

    first.wait()

    def remote(src, dst, send_sem, recv_sem, *device):
        return pltpu.make_async_remote_copy(
            src_ref=src, dst_ref=dst, send_sem=send_sem, recv_sem=recv_sem,
            device_id=device, device_id_type=MESH,
        )

    sent = []

    def go(copy):
        copy.start()
        sent.append(copy)

    groups = (row, over)
    limit = ((4, 3), (3, 4))
    step_to = (right, left)

    def origin(way, hop):
        return lax.rem(col + (cols - hop if way == 0 else hop), cols)

    def chunk_at(group, source, chunk):
        return praw.at[group, source, pl.ds(BS * chunk, BS), :]

    def ring(place, kind, chunk, way, hop):
        return remote(
            place, place, send.at[kind, chunk, way, hop], recv.at[kind, chunk, way, hop], layer, row, step_to[way]
        )

    def passed(place, kind, chunk, way, hop):
        return remote(
            place, place, far.at[0, kind, chunk, way, hop], far.at[1, kind, chunk, way, hop], layer, mate, col
        )

    def across(place, chunk, way=0):
        return remote(place, place, near.at[way, chunk], near.at[way + 1, chunk], layer, over, col)

    def beside(place, kind, chunk):
        return remote(place, place, near.at[2 + 2 * kind, chunk], near.at[3 + 2 * kind, chunk], layer, mate, col)

    for chunk in range(2):
        place = chunk_at(row, col, chunk)
        go(across(place, chunk))
        for way in range(2):
            go(ring(place, 0, chunk, way, 0))
    for copy in lows + trailing:
        copy.start()
    for chunk in range(2):
        go(beside(chunk_at(row, col, chunk), 0, chunk))
    for copy in ups:
        copy.wait()

    def up_copy(block, way, group, *device):
        place = uraw.at[group, block]
        return remote(place, place, up_send.at[way, block], up_recv.at[way, block], *device)

    for block in range(2):
        go(up_copy(block, 0, row, layer, over, col))

    for kind, chunk, hop in ORDER:
        if hop == 0:
            place = chunk_at(over, col, chunk)
            across(place, chunk).wait_recv()
            for way in range(2):
                go(ring(place, 1, chunk, way, 0))
            go(beside(place, 1, chunk))
            continue
        for way in range(2):
            if hop > limit[chunk][way]:
                continue
            place = chunk_at(groups[kind], origin(way, hop), chunk)
            if kind == 1 and hop == 4:
                across(place, chunk, 6).wait_recv()
            else:
                ring(place, kind, chunk, way, hop - 1).wait_recv()
            if hop < (limit[chunk][way], 3)[kind]:
                go(ring(place, kind, chunk, way, hop))
            if kind == 0 and hop == 4:
                go(across(place, chunk, 6))
                if chunk == 1:
                    go(up_copy(2, 0, row, layer, over, col))
            go(passed(place, kind, chunk, way, hop - 1))

    def low_part(kind, source):
        return lraw.at[source, pl.ds(384 * kind, 384), :]

    for copy in lows:
        copy.wait()
    for kind in range(2):
        for way in range(2):
            half = low_part(kind, col)
            go(remote(
                half, half, lo_send.at[kind, way, 0], lo_recv.at[kind, way, 0],
                layer, row, step_to[way],
            ))

    def low_ring(place, kind, way, hop):
        return remote(
            place, place, lo_send.at[kind, way, hop], lo_recv.at[kind, way, hop], layer, row, step_to[way]
        )

    def low_hop(kind, hop):
        for way in range(2):
            if hop > limit[kind][way]:
                continue
            place = low_part(kind, origin(way, hop))
            low_ring(place, kind, way, hop - 1).wait_recv()
            if hop < limit[kind][way]:
                low_ring(place, kind, way, hop).start()

    for block in range(3):
        go(up_copy(block, 1, row, layer, mate, col))

    mates = (mate, rows_n - 1 - row)
    for kind, chunk, hop in ORDER:
        if hop == 0:
            beside(chunk_at(mates[1], col, chunk), 1, chunk).wait_recv()
            beside(chunk_at(mates[0], col, chunk), 0, chunk).wait_recv()
            continue
        for way in range(2):
            if hop <= limit[chunk][way]:
                place = chunk_at(mates[kind], origin(way, hop), chunk)
                passed(place, kind, chunk, way, hop - 1).wait_recv()

    def up_over():
        for block in range(3):
            up_copy(block, 0, over, layer, over, col).wait_recv()
            up_copy(block, 2, over, layer, mate, col).start()

    def up_here():
        for block in range(3):
            for k in range(2):
                up_copy(block, 1 + k, mates[k], layer, mate, col).wait_recv()
        for i in range(8):
            for b in range(3):
                work[i * BS : (i + 1) * BS, 1024 + b * BS : 1024 + (b + 1) * BS] = (
                    uraw[i // 2, b, (i % 2) * BS : (i % 2 + 1) * BS, :] * filled(i, 8 * (b + 1) + col)
                )
        for k in range(LATE):
            begin, end = k * BS, (k + 1) * BS
            work[end:1024, 1024:1408] -= bulk(work[end:1024, begin:end], work[begin:end, 1024:1408])

    def filled(i, j):
        return mask_ref[i, j].astype(jnp.float32)

    @pl.loop(0, 8)
    def _(i):
        group, part = i // 2, pl.multiple_of(lax.rem(i, 2) * BS, BS)
        here = pl.ds(pl.multiple_of(i * BS, BS), BS)
        for j in range(8):
            work[here, j * BS : (j + 1) * BS] = praw[group, j, pl.ds(part, BS), :] * filled(i, j)

    @pl.loop(0, 8)
    def _(j):
        here = pl.ds(pl.multiple_of(j * BS, BS), BS)
        inv[j] = invert(work[here, here], unit, scaled)
        pl.when(j == 0)(up_over)
        pl.when(j == LATE)(up_here)
        for k in range(7):

            @pl.when(j == k)
            def _(k=k):
                begin, end = k * BS, (k + 1) * BS
                factors = bulk(work[end:1024, begin:end], inv[k])
                work[end:1024, begin:end] = factors
                last = 1408 if k >= LATE else 1024
                for start in range(end, last, 256):
                    stop = min(start + 256, last)
                    work[end:1024, start:stop] -= bulk(factors, work[begin:end, start:stop])

        for hop in range(1, 5):
            for kind in range(2 if hop < 4 else 1):

                @pl.when(j == 2 * hop - 2 + kind)
                def _(kind=kind, hop=hop):
                    low_hop(kind, hop)

    for m in range(4):
        first, second = inv[2 * m], inv[2 * m + 1]
        between = work[256 * m : 256 * m + BS, 256 * m + BS : 256 * m + 256]
        pairs[m, 0:BS, 0:BS] = first
        pairs[m, BS:256, BS:256] = second
        pairs[m, BS:256, 0:BS] = jnp.zeros((BS, BS), jnp.float32)
        pairs[m, 0:BS, BS:256] = -bulk(first, bulk(between, second))
    up_high[...], up_low[...] = halves(work[:, 1024:1408])

    def solve(supers):
        for a in supers:
            for h in range(2):
                here = slice(256 * a + BS * h, 256 * a + BS * (h + 1))
                for j in range(8):
                    low[here, j * BS : (j + 1) * BS] = lraw[j, here, :] * filled(8 * (a + 1) + 2 * row + h, j)
        for m in range(4):
            begin, end = 256 * m, 256 * m + 256
            pair = halves(pairs[m])
            above = halves(work[:begin, begin:end]) if m else None
            for a in supers:
                here = slice(256 * a, 256 * a + 256)
                value = low[here, begin:end]
                if m:
                    value = value - passes((low_high[here, :begin], low_low[here, :begin]), above)
                value = passes(halves(value), pair)
                low[here, begin:end] = value
                low_high[here, begin:end], low_low[here, begin:end] = halves(value)
        for a in supers:
            here = slice(256 * a, 256 * a + 256)
            term = passes((low_high[here, :], low_low[here, :]), (up_high[...], up_low[...]))
            for h in range(2):
                for b in range(3):
                    block = rest[a, b, BS * h : BS * (h + 1), :]
                    block = block * filled(8 * (a + 1) + 2 * row + h, 8 * (b + 1) + col)
                    block = block - term[BS * h : BS * (h + 1), BS * b : BS * (b + 1)]
                    tail[a, BS * h : BS * (h + 1), BS * b : BS * (b + 1)] = block
            for d in range(1, layers):
                other = lax.rem(layer + d, layers)
                go(remote(
                    tail.at[a, pl.ds(pl.multiple_of(other * 32, 32), 32), :], got.at[d, a],
                    sum_send.at[d, a], sum_recv.at[d, a], other, row, col,
                ))

    for copy in trailing:
        copy.wait()
    solve((0,))
    low_hop(1, 4)
    solve((1, 2))

    mine, there = pl.ds(pl.multiple_of(row * 256, 256), 256), pl.ds(pl.multiple_of(col * BS, BS), BS)
    out_ref[pl.ds(0, 256, stride=4), :] = work[mine, there]
    for b in range(3):
        out_ref[pl.ds(b + 1, 256, stride=4), :] = work[mine, 1024 + BS * b : 1024 + BS * (b + 1)]
    for a in range(3):
        base = 1024 * (a + 1)
        out_ref[pl.ds(base, 256, stride=4), :] = low[256 * a : 256 * (a + 1), there]
        for b in range(3):
            out_ref[pl.ds(base + b + 1, 256, stride=4), :] = tail[a, :, BS * b : BS * (b + 1)]

    ours = pl.ds(pl.multiple_of(layer * 32, 32), 32)
    for a in range(3):
        for d in range(1, layers):
            place = got.at[d, a]
            remote(place, place, sum_send.at[d, a], sum_recv.at[d, a], layer, row, col).wait_recv()
        total = tail[a, ours, :]
        for d in range(1, layers):
            total = total + got[d, a]
        for b in range(3):
            anc_ref[a, b] = total[:, BS * b : BS * (b + 1)]

    for copy in sent:
        copy.wait_send()
    for block in range(3):
        up_copy(block, 2, over, layer, mate, col).wait_send()
    for kind in range(2):
        for way in range(2):
            for hop in range(1, limit[kind][way]):
                low_ring(low_part(kind, col), kind, way, hop).wait_send()


def handed_on(staged_ref, out_ref, sems):
    copies = [
        pltpu.make_async_copy(staged_ref.at[pl.ds(1024 * k, 1024)], out_ref.at[pl.ds(1024 * k, 1024)], sems.at[k])
        for k in range(4)
    ]
    for copy in copies:
        copy.start()
    for copy in copies:
        copy.wait()


def on_device(front_blocks, fill_mask):
    dma = pltpu.SemaphoreType.DMA
    vmem = lambda *shape: pltpu.VMEM(shape, jnp.float32)
    narrow = lambda *shape: pltpu.VMEM(shape, jnp.bfloat16)
    factored, ancestor = pl.pallas_call(
        kernel,
        out_shape=(
            pltpu.VMEM((4096, 128), jnp.float32),
            jax.ShapeDtypeStruct((3, 3, 32, 128), jnp.float32),
        ),
        in_specs=[pl.BlockSpec(memory_space=pl.ANY), pl.BlockSpec(memory_space=pltpu.SMEM)],
        out_specs=(pl.BlockSpec(memory_space=pltpu.VMEM), pl.BlockSpec(memory_space=pltpu.VMEM)),
        scratch_shapes=[
            vmem(4, 8, 256, 128), vmem(4, 3, 256, 128), vmem(8, 768, 128),
            vmem(3, 3, 256, 128), vmem(1024, 1408), vmem(768, 1024), narrow(768, 1024), narrow(768, 1024),
            narrow(1024, 384), narrow(1024, 384), vmem(4, 256, 256), vmem(3, 256, 384), vmem(8, 3, 32, 384),
            vmem(8, 128, 128), vmem(128, 128), vmem(128, 128),
            dma((2, 2, 2, 4)), dma((2, 2, 2, 4)), dma((8, 2)), dma((2, 2, 2, 2, 4)),
            dma((3, 3)), dma((3, 3)), dma((2, 2, 4)), dma((2, 2, 4)), dma((8, 3)), dma((8, 3)), dma((16,)),
        ],
        compiler_params=pltpu.CompilerParams(
            collective_id=0, has_side_effects=True, vmem_limit_bytes=60 * 1024 * 1024
        ),
        name="eliminate",
    )(front_blocks[0], fill_mask)
    factored = pl.pallas_call(
        handed_on, out_shape=jax.ShapeDtypeStruct((4096, 128), jnp.float32),
        in_specs=[pl.BlockSpec(memory_space=pltpu.VMEM)], out_specs=pl.BlockSpec(memory_space=pl.ANY),
        scratch_shapes=[dma((4,))], name="hand_on",
    )(pltpu.with_memory_space_constraint(factored, pltpu.VMEM))
    return factored.reshape(1, 4, 256, 4, 128), ancestor.transpose(0, 2, 1, 3).reshape(3, 1, 1, 32, 3, 128)


def solution(mesh):
    split = P("layer", None, "prow", None, "pcol")
    return jax.shard_map(
        on_device,
        mesh=mesh,
        in_specs=(split, P()),
        out_specs=(split, P(None, "prow", "layer", None, None, "pcol")),
        check_vma=False,
    )
```

```python
import jax
import jax.numpy as jnp
from jax import lax
from jax.experimental import pallas as pl
from jax.experimental.pallas import tpu as pltpu
from jax.sharding import PartitionSpec as P

BS = 128
WIDE = 16
SPAN = 32
LATE = 1
MESH = pl.DeviceIdType.MESH
ORDER = (
    (0, 0, 1), (0, 1, 1), (1, 0, 0), (0, 0, 2), (0, 1, 2), (1, 1, 0), (1, 0, 1), (0, 0, 3), (0, 1, 3), (1, 1, 1),
    (1, 0, 2), (0, 0, 4), (0, 1, 4), (1, 1, 2), (1, 0, 3), (1, 1, 3), (1, 0, 4), (1, 1, 4),
)


def dot(left, right, dims=((1,), (0,)), precision=lax.Precision.HIGHEST):
    return lax.dot_general(
        left, right, (dims, ((), ())), precision=precision, preferred_element_type=jnp.float32
    )


def bulk(left, right):
    return dot(left, right, precision=lax.Precision.HIGH)


def lanes_of(block, column):
    return jnp.broadcast_to(block[:, column : column + 1], (WIDE, BS))


def row_of(block, row):
    return jnp.broadcast_to(block[row : row + 1, :], (WIDE, BS))


def invert(pivot, unit_ref, scaled_ref):
    gram = dot(pivot, pivot, ((1,), (1,)))
    count, span = BS // WIDE, SPAN // WIDE
    groups = [gram[WIDE * p : WIDE * (p + 1), :] for p in range(count)]
    lane = lax.broadcasted_iota(jnp.int32, (WIDE, BS), 1)
    sub = lax.broadcasted_iota(jnp.int32, (WIDE, BS), 0)
    raw, done = [], []
    for p in range(count):
        start, stop = WIDE * p, WIDE * (p + 1)
        if p and p % span == 0:
            term = dot(jnp.concatenate(raw, 0), jnp.concatenate(done, 0), ((0,), (0,)))
            raw, done = [], []
            for q in range(p, count):
                kept = jnp.where((lane >= start - SPAN) & (lane < start), 0.0, groups[q])
                groups[q] = kept - term[WIDE * q : WIDE * (q + 1), :]
        rows = groups[p]
        raw.append(rows)
        own = (lane >= start) & (lane < stop)
        eye = jnp.where(lane - start == sub, 1.0, 0.0)
        columns = [lanes_of(rows, start + j) for j in range(WIDE)]
        unit_ref[start:stop, :] = jnp.where(lane < start, rows, eye)
        rows = jnp.where(own, eye, rows)
        for k in range(0, WIDE, 2):
            first, second = columns[k], columns[k + 1]
            a, b = row_of(first, k), row_of(second, k)
            c, d = row_of(first, k + 1), row_of(second, k + 1)
            scale = 1.0 / (a * d - b * c)
            at, after = sub == k, sub == k + 1
            left = jnp.where(at, -d, jnp.where(after, c, first * d - second * c))
            right = jnp.where(at, b, jnp.where(after, -a, second * a - first * b))

            def cleared(block, k=k, pair=at | after, left=left, right=right, scale=scale):
                term = left * row_of(block, k) + right * row_of(block, k + 1)
                return jnp.where(pair, 0.0, block) - term * scale

            rows = cleared(rows)
            for j in range(k + 2, WIDE):
                columns[j] = cleared(columns[j])
        end = (p // span + 1) * span
        done.append(jnp.where((lane < stop) | (lane >= WIDE * end), rows, 0.0))
        scaled_ref[start:stop, :] = jnp.where(lane < stop, rows, 0.0)
        tops = [row_of(rows, k) for k in range(WIDE)]
        for q in range(p + 1, end):
            terms = [lanes_of(groups[q], start + k) * tops[k] for k in range(WIDE)]
            while len(terms) > 1:
                terms = [terms[i] + terms[i + 1] for i in range(0, len(terms), 2)]
            groups[q] = jnp.where(own, 0.0, groups[q]) - terms[0]
    right = dot(unit_ref[...], pivot)
    return dot(right, scaled_ref[...], ((0,), (0,)))


def halves(value):
    high = value.astype(jnp.bfloat16)
    return high, (value - high.astype(jnp.float32)).astype(jnp.bfloat16)


def passes(left, right):
    def one(a, b):
        return jnp.dot(a, b, preferred_element_type=jnp.float32)

    return one(left[0], right[0]) + (one(left[0], right[1]) + one(left[1], right[0]))


def kernel(
    x_ref, mask_ref, out_ref, anc_ref,
    praw, uraw, lraw, rest, work, low, low_high, low_low, up_high, up_low, pairs, tail, got, inv, unit, scaled,
    send, recv, near, far, up_send, up_recv, lo_send, lo_recv, sum_send, sum_recv, local,
):
    layer, row, col = lax.axis_index("layer"), lax.axis_index("prow"), lax.axis_index("pcol")
    cols, rows_n, layers = 8, 4, 8
    mate = row + 1 - 2 * lax.rem(row, 2)
    over = lax.rem(row + 2, rows_n)
    right, left = lax.rem(col + 1, cols), lax.rem(col + cols - 1, cols)

    first = pltpu.make_async_copy(x_ref.at[0, :, 0, :], praw.at[row, col], local.at[0])
    ups, lows = [], []
    for a in range(3):
        ups.append(pltpu.make_async_copy(x_ref.at[0, :, a + 1, :], uraw.at[row, a], local.at[4 + a]))
        lows.append(pltpu.make_async_copy(x_ref.at[a + 1, :, 0, :], lraw.at[col, pl.ds(256 * a, 256), :], local.at[1 + a]))
    trailing = [
        pltpu.make_async_copy(x_ref.at[a + 1, :, b + 1, :], rest.at[a, b], local.at[7 + 3 * a + b])
        for a in range(3)
        for b in range(3)
    ]
    first.start()
    for copy in ups:
        copy.start()

    barrier = pltpu.get_barrier_semaphore()

    def greet(*device):
        pl.semaphore_signal(barrier, inc=1, device_id=device, device_id_type=MESH)

    greet(layer, mate, col)
    greet(layer, over, col)
    greet(layer, row, right)
    greet(layer, row, left)
    for d in range(1, layers):
        greet(lax.rem(layer + d, layers), row, col)
    pl.semaphore_wait(barrier, 4 + layers - 1)

    first.wait()

    def remote(src, dst, send_sem, recv_sem, *device):
        return pltpu.make_async_remote_copy(
            src_ref=src, dst_ref=dst, send_sem=send_sem, recv_sem=recv_sem,
            device_id=device, device_id_type=MESH,
        )

    sent = []

    def go(copy):
        copy.start()
        sent.append(copy)

    groups = (row, over)
    limit = ((4, 3), (3, 4))
    step_to = (right, left)

    def origin(way, hop):
        return lax.rem(col + (cols - hop if way == 0 else hop), cols)

    def chunk_at(group, source, chunk):
        return praw.at[group, source, pl.ds(BS * chunk, BS), :]

    def ring(place, kind, chunk, way, hop):
        return remote(
            place, place, send.at[kind, chunk, way, hop], recv.at[kind, chunk, way, hop], layer, row, step_to[way]
        )

    def passed(place, kind, chunk, way, hop):
        return remote(
            place, place, far.at[0, kind, chunk, way, hop], far.at[1, kind, chunk, way, hop], layer, mate, col
        )

    def across(place, chunk, way=0):
        return remote(place, place, near.at[way, chunk], near.at[way + 1, chunk], layer, over, col)

    def beside(place, kind, chunk):
        return remote(place, place, near.at[2 + 2 * kind, chunk], near.at[3 + 2 * kind, chunk], layer, mate, col)

    for chunk in range(2):
        place = chunk_at(row, col, chunk)
        go(across(place, chunk))
        for way in range(2):
            go(ring(place, 0, chunk, way, 0))
    for copy in lows + trailing:
        copy.start()
    for chunk in range(2):
        go(beside(chunk_at(row, col, chunk), 0, chunk))
    for copy in ups:
        copy.wait()

    def up_copy(block, way, group, *device):
        place = uraw.at[group, block]
        return remote(place, place, up_send.at[way, block], up_recv.at[way, block], *device)

    for block in range(2):
        go(up_copy(block, 0, row, layer, over, col))

    for kind, chunk, hop in ORDER:
        if hop == 0:
            place = chunk_at(over, col, chunk)
            across(place, chunk).wait_recv()
            for way in range(2):
                go(ring(place, 1, chunk, way, 0))
            go(beside(place, 1, chunk))
            continue
        for way in range(2):
            if hop > limit[chunk][way]:
                continue
            place = chunk_at(groups[kind], origin(way, hop), chunk)
            if kind == 1 and hop == 4:
                across(place, chunk, 6).wait_recv()
            else:
                ring(place, kind, chunk, way, hop - 1).wait_recv()
            if hop < (limit[chunk][way], 3)[kind]:
                go(ring(place, kind, chunk, way, hop))
            if kind == 0 and hop == 4:
                go(across(place, chunk, 6))
                if chunk == 1:
                    go(up_copy(2, 0, row, layer, over, col))
            go(passed(place, kind, chunk, way, hop - 1))

    def low_part(kind, source):
        return lraw.at[source, pl.ds(384 * kind, 384), :]

    for copy in lows:
        copy.wait()
    for kind in range(2):
        for way in range(2):
            half = low_part(kind, col)
            go(remote(
                half, half, lo_send.at[kind, way, 0], lo_recv.at[kind, way, 0],
                layer, row, step_to[way],
            ))

    def low_ring(place, kind, way, hop):
        return remote(
            place, place, lo_send.at[kind, way, hop], lo_recv.at[kind, way, hop], layer, row, step_to[way]
        )

    def low_hop(kind, hop):
        for way in range(2):
            if hop > limit[kind][way]:
                continue
            place = low_part(kind, origin(way, hop))
            low_ring(place, kind, way, hop - 1).wait_recv()
            if hop < limit[kind][way]:
                low_ring(place, kind, way, hop).start()

    for block in range(3):
        go(up_copy(block, 1, row, layer, mate, col))

    mates = (mate, rows_n - 1 - row)
    for kind, chunk, hop in ORDER:
        if hop == 0:
            beside(chunk_at(mates[1], col, chunk), 1, chunk).wait_recv()
            beside(chunk_at(mates[0], col, chunk), 0, chunk).wait_recv()
            continue
        for way in range(2):
            if hop <= limit[chunk][way]:
                place = chunk_at(mates[kind], origin(way, hop), chunk)
                passed(place, kind, chunk, way, hop - 1).wait_recv()

    def up_over():
        for block in range(3):
            up_copy(block, 0, over, layer, over, col).wait_recv()
            up_copy(block, 2, over, layer, mate, col).start()

    def up_here():
        for block in range(3):
            for k in range(2):
                up_copy(block, 1 + k, mates[k], layer, mate, col).wait_recv()
        for i in range(8):
            for b in range(3):
                work[i * BS : (i + 1) * BS, 1024 + b * BS : 1024 + (b + 1) * BS] = (
                    uraw[i // 2, b, (i % 2) * BS : (i % 2 + 1) * BS, :] * filled(i, 8 * (b + 1) + col)
                )
        for k in range(LATE):
            begin, end = k * BS, (k + 1) * BS
            work[end:1024, 1024:1408] -= bulk(work[end:1024, begin:end], work[begin:end, 1024:1408])

    def filled(i, j):
        return mask_ref[i, j].astype(jnp.float32)

    @pl.loop(0, 8)
    def _(i):
        group, part = i // 2, pl.multiple_of(lax.rem(i, 2) * BS, BS)
        here = pl.ds(pl.multiple_of(i * BS, BS), BS)
        for j in range(8):
            work[here, j * BS : (j + 1) * BS] = praw[group, j, pl.ds(part, BS), :] * filled(i, j)

    @pl.loop(0, 8)
    def _(j):
        here = pl.ds(pl.multiple_of(j * BS, BS), BS)
        inv[j] = invert(work[here, here], unit, scaled)
        pl.when(j == 0)(up_over)
        pl.when(j == LATE)(up_here)
        for k in range(7):

            @pl.when(j == k)
            def _(k=k):
                begin, end = k * BS, (k + 1) * BS
                factors = bulk(work[end:1024, begin:end], inv[k])
                work[end:1024, begin:end] = factors
                last = 1408 if k >= LATE else 1024
                for start in range(end, last, 256):
                    stop = min(start + 256, last)
                    work[end:1024, start:stop] -= bulk(factors, work[begin:end, start:stop])

        for hop in range(1, 5):
            for kind in range(2 if hop < 4 else 1):

                @pl.when(j == 2 * hop - 2 + kind)
                def _(kind=kind, hop=hop):
                    low_hop(kind, hop)

    for m in range(4):
        first, second = inv[2 * m], inv[2 * m + 1]
        between = work[256 * m : 256 * m + BS, 256 * m + BS : 256 * m + 256]
        pairs[m, 0:BS, 0:BS] = first
        pairs[m, BS:256, BS:256] = second
        pairs[m, BS:256, 0:BS] = jnp.zeros((BS, BS), jnp.float32)
        pairs[m, 0:BS, BS:256] = -bulk(first, bulk(between, second))
    up_high[...], up_low[...] = halves(work[:, 1024:1408])

    def solve(supers):
        for a in supers:
            for h in range(2):
                here = slice(256 * a + BS * h, 256 * a + BS * (h + 1))
                for j in range(8):
                    low[here, j * BS : (j + 1) * BS] = lraw[j, here, :] * filled(8 * (a + 1) + 2 * row + h, j)
        for m in range(4):
            begin, end = 256 * m, 256 * m + 256
            pair = halves(pairs[m])
            above = halves(work[:begin, begin:end]) if m else None
            for a in supers:
                here = slice(256 * a, 256 * a + 256)
                value = low[here, begin:end]
                if m:
                    value = value - passes((low_high[here, :begin], low_low[here, :begin]), above)
                value = passes(halves(value), pair)
                low[here, begin:end] = value
                low_high[here, begin:end], low_low[here, begin:end] = halves(value)
        for a in supers:
            here = slice(256 * a, 256 * a + 256)
            term = passes((low_high[here, :], low_low[here, :]), (up_high[...], up_low[...]))
            for h in range(2):
                for b in range(3):
                    block = rest[a, b, BS * h : BS * (h + 1), :]
                    block = block * filled(8 * (a + 1) + 2 * row + h, 8 * (b + 1) + col)
                    block = block - term[BS * h : BS * (h + 1), BS * b : BS * (b + 1)]
                    tail[a, BS * h : BS * (h + 1), BS * b : BS * (b + 1)] = block
            for d in (4, 3, 5, 2, 6, 1, 7):
                other = lax.rem(layer + d, layers)
                go(remote(
                    tail.at[a, pl.ds(pl.multiple_of(other * 32, 32), 32), :], got.at[d, a],
                    sum_send.at[d, a], sum_recv.at[d, a], other, row, col,
                ))

    for copy in trailing:
        copy.wait()
    solve((0,))
    low_hop(1, 4)
    solve((1,))
    solve((2,))

    mine, there = pl.ds(pl.multiple_of(row * 256, 256), 256), pl.ds(pl.multiple_of(col * BS, BS), BS)
    out_ref[pl.ds(0, 256, stride=4), :] = work[mine, there]
    for b in range(3):
        out_ref[pl.ds(b + 1, 256, stride=4), :] = work[mine, 1024 + BS * b : 1024 + BS * (b + 1)]
    for a in range(3):
        base = 1024 * (a + 1)
        out_ref[pl.ds(base, 256, stride=4), :] = low[256 * a : 256 * (a + 1), there]
        for b in range(3):
            out_ref[pl.ds(base + b + 1, 256, stride=4), :] = tail[a, :, BS * b : BS * (b + 1)]

    ours = pl.ds(pl.multiple_of(layer * 32, 32), 32)
    for a in range(3):
        for d in range(1, layers):
            place = got.at[d, a]
            remote(place, place, sum_send.at[d, a], sum_recv.at[d, a], layer, row, col).wait_recv()
        total = tail[a, ours, :]
        for d in range(1, layers):
            total = total + got[d, a]
        for b in range(3):
            anc_ref[a, b] = total[:, BS * b : BS * (b + 1)]

    for copy in sent:
        copy.wait_send()
    for block in range(3):
        up_copy(block, 2, over, layer, mate, col).wait_send()
    for kind in range(2):
        for way in range(2):
            for hop in range(1, limit[kind][way]):
                low_ring(low_part(kind, col), kind, way, hop).wait_send()


def handed_on(staged_ref, out_ref, sems):
    copies = [
        pltpu.make_async_copy(staged_ref.at[pl.ds(1024 * k, 1024)], out_ref.at[pl.ds(1024 * k, 1024)], sems.at[k])
        for k in range(4)
    ]
    for copy in copies:
        copy.start()
    for copy in copies:
        copy.wait()


def on_device(front_blocks, fill_mask):
    dma = pltpu.SemaphoreType.DMA
    vmem = lambda *shape: pltpu.VMEM(shape, jnp.float32)
    narrow = lambda *shape: pltpu.VMEM(shape, jnp.bfloat16)
    factored, ancestor = pl.pallas_call(
        kernel,
        out_shape=(
            pltpu.VMEM((4096, 128), jnp.float32),
            jax.ShapeDtypeStruct((3, 3, 32, 128), jnp.float32),
        ),
        in_specs=[pl.BlockSpec(memory_space=pl.ANY), pl.BlockSpec(memory_space=pltpu.SMEM)],
        out_specs=(pl.BlockSpec(memory_space=pltpu.VMEM), pl.BlockSpec(memory_space=pltpu.VMEM)),
        scratch_shapes=[
            vmem(4, 8, 256, 128), vmem(4, 3, 256, 128), vmem(8, 768, 128),
            vmem(3, 3, 256, 128), vmem(1024, 1408), vmem(768, 1024), narrow(768, 1024), narrow(768, 1024),
            narrow(1024, 384), narrow(1024, 384), vmem(4, 256, 256), vmem(3, 256, 384), vmem(8, 3, 32, 384),
            vmem(8, 128, 128), vmem(128, 128), vmem(128, 128),
            dma((2, 2, 2, 4)), dma((2, 2, 2, 4)), dma((8, 2)), dma((2, 2, 2, 2, 4)),
            dma((3, 3)), dma((3, 3)), dma((2, 2, 4)), dma((2, 2, 4)), dma((8, 3)), dma((8, 3)), dma((16,)),
        ],
        compiler_params=pltpu.CompilerParams(
            collective_id=0, has_side_effects=True, vmem_limit_bytes=60 * 1024 * 1024
        ),
        name="eliminate",
    )(front_blocks[0], fill_mask)
    factored = pl.pallas_call(
        handed_on, out_shape=jax.ShapeDtypeStruct((4096, 128), jnp.float32),
        in_specs=[pl.BlockSpec(memory_space=pltpu.VMEM)], out_specs=pl.BlockSpec(memory_space=pl.ANY),
        scratch_shapes=[dma((4,))], name="hand_on",
    )(pltpu.with_memory_space_constraint(factored, pltpu.VMEM))
    return factored.reshape(1, 4, 256, 4, 128), ancestor.transpose(0, 2, 1, 3).reshape(3, 1, 1, 32, 3, 128)


def solution(mesh):
    split = P("layer", None, "prow", None, "pcol")
    return jax.shard_map(
        on_device,
        mesh=mesh,
        in_specs=(split, P()),
        out_specs=(split, P(None, "prow", "layer", None, None, "pcol")),
        check_vma=False,
    )
```
